32 devices in a mesh: dp: 8 (over z, y), group: 4 (over x, core).
Axes of the slice: x: 2, y: 2, z: 4, core: 2. Of those that a mesh axis runs over, the one named last changes fastest.
Arguments:
- waveform: bfloat16 [128, 2560], P(('dp', 'group')), may hold values from -6 to 6
- lengths: int32 [128], P(('dp', 'group')), may hold values from 1280 to 2560
- packing: int32 [128], P(('dp', 'group')), may hold values from 0 to 15, as said below
- first_weight: bfloat16 [512, 10], P('dp'), may hold values from -2 to 2
- norm_gain: float32 [512], replicated, may hold values from 0.25 to 1.75
- norm_bias: float32 [512], replicated, may hold values from -3 to 3
- conv_weight: bfloat16 [512, 1536], P('dp'), may hold values from -0.15625 to 0.15625
- grad_features: bfloat16 [128, 255, 512], P(('dp', 'group')), may hold values from -0.25 to 0.25
Outputs:
- features: bfloat16 [128, 255, 512], P(('dp', 'group'))
- grad_conv: float32 [512, 1536], P('dp')
- grad_first: float32 [512, 10], P('dp')
- grad_gain: float32 [512], replicated
- grad_bias: float32 [512], replicated
The draws below stay inside these ranges and needn't reach their ends.
Inputs may be any that keep to these rules, and one draw needn't show every extreme that they name: `packing`: within each index of dp the 16 rows form a permutation of the positions of that index's block; position p lies on the device of group index p // 4 of the same dp index. Each device sends an even number of its rows to each device of its group, at most 2 to one device, and exactly 2 to some.
All inputs are finite; a program needn't handle non-finite values.
Results may differ from the reference program's by a relative error of at most 0.0057.
Values may be sent and summed in bfloat16 or wider, within the bound.
A program may use at most 64 MiB of HBM per device.

```python
import jax
import jax.numpy as jnp
from jax import lax

C = 512
CAP = 2560
ROWS_DEV = 4
F1 = 255
UTTS = 128
N_DP = 8
N_GROUP = 4


def draw_packing(key, part):
    block_rows = N_GROUP * ROWS_DEV
    key_rows, key_offset, key_label, key_slot = jax.random.split(key, 4)
    row_order = jax.vmap(lambda sub: jax.random.permutation(sub, ROWS_DEV))(jax.random.split(key_rows, N_DP * N_GROUP))
    row_order = row_order.reshape(N_DP, N_GROUP, ROWS_DEV)
    shift_amount = row_order // 2 % N_GROUP
    offset = jax.random.randint(key_offset, (N_DP, 1, 1), 0, N_GROUP)
    relabel = jax.vmap(lambda sub: jax.random.permutation(sub, N_GROUP))(jax.random.split(key_label, N_DP))
    source = jnp.arange(N_GROUP)[None, :, None]
    cycled = (source + shift_amount + offset) % N_GROUP
    target = jnp.take_along_axis(relabel, cycled.reshape(N_DP, block_rows), axis=1)
    positions = jnp.arange(block_rows)
    same_target = target[:, :, None] == target[:, None, :]
    earlier = positions[:, None] > positions[None, :]
    rank_among = jnp.sum((same_target & earlier[None]).astype(jnp.int32), axis=2)
    slot_perm = jax.vmap(lambda sub: jax.random.permutation(sub, ROWS_DEV))(jax.random.split(key_slot, N_DP * N_GROUP))
    slot_perm = slot_perm.reshape(N_DP, block_rows)
    slot_value = jnp.take_along_axis(slot_perm, target * ROWS_DEV + rank_among, axis=1)
    return (target * ROWS_DEV + slot_value).reshape(N_DP * block_rows).astype(jnp.int32)


def touch_ends(entries, own_key, low, largest):
    spot = [jax.random.randint(jax.random.fold_in(own_key, axis), (), 0, length) for axis, length in enumerate(entries.shape)]
    main_axis = entries.shape.index(max(entries.shape))
    neighbour = spot[:main_axis] + [(spot[main_axis] + 1) % entries.shape[main_axis]] + spot[main_axis + 1:]
    return entries.at[tuple(spot)].set(low).at[tuple(neighbour)].set(largest)


def strengthened(drawn, rng, source, target, parts, factor):
    def block_of(dim):
        return (jnp.arange(drawn.shape[dim]) // (drawn.shape[dim] // parts)).reshape((-1,) + (1,) * (drawn.ndim - 1 - dim))

    first = jax.random.permutation(rng, parts)[block_of(target)]
    other_side = (block_of(target) + parts // 2) % parts
    return jnp.where((block_of(source) == first) | (block_of(source) == other_side), factor * drawn, drawn)


def levels(own_key, shape, cuts, smallest, largest):
    gain, own = 1.0, jax.random.fold_in(own_key, 6)
    for axis_at, parts in cuts:
        draws = jnp.exp(jax.random.uniform(jax.random.fold_in(own, axis_at), (parts,), jnp.float32, smallest / len(cuts), largest / len(cuts)))
        gain = gain * jnp.repeat(draws, shape[axis_at] // parts).reshape([-1 if axis == axis_at else 1 for axis in range(len(shape))])
    return gain


def gaussian(own_key, extent, width, bound, shards=(), kind=jnp.bfloat16):
    entries = jax.random.normal(own_key, extent, jnp.float32) * width
    if len(shards) > 0:
        entries = levels(own_key, extent, shards, -0.22, 0.18) * entries
    return jnp.clip(entries, min=-bound, max=bound).astype(kind)


def gaussian_with(stream_key, shape, spread, bound, pieces, heavy, held_as=jnp.bfloat16):
    values = spread * jax.random.normal(stream_key, shape, jnp.float32)
    if pieces:
        values = values * levels(stream_key, shape, pieces, -0.22, 0.18)
    return jnp.clip(strengthened(values, jax.random.fold_in(stream_key, 3), *heavy), -bound, bound).astype(held_as)


def setup_inputs(seed: int = 0) -> dict:
    streams_of = jax.random.split(jax.random.key(seed), 9)
    waveform = gaussian(streams_of[0], (UTTS, CAP), 1.0, 6.0, ((0, 32),))
    lengths = touch_ends(jax.random.randint(streams_of[1], (UTTS,), CAP // 2, CAP + 1), jax.random.fold_in(streams_of[1], 1), CAP // 2, CAP).astype(jnp.int32)
    packing = draw_packing(jax.random.fold_in(streams_of[8], 71), 0)
    first_weight = gaussian(streams_of[3], (C, 10), 10 ** -0.5, 2.0, ((0, 8),))
    norm_gain = jnp.clip(1.0 + 0.15 * jax.random.normal(streams_of[4], (C,), jnp.float32), 0.25, 1.75)
    norm_bias = gaussian(streams_of[5], (C,), 0.5, 3.0, (), jnp.float32)
    conv_weight = gaussian(streams_of[6], (C, 3 * C), (3 * C) ** -0.5, 0.15625, ((0, 8),))
    grad_features = gaussian_with(streams_of[7], (UTTS, F1, C), (4.0 * (UTTS * F1) ** -0.5), 0.25, ((0, 32),), (0, 2, 32, 2.75))
    return {"waveform": waveform, "lengths": lengths, "packing": packing, "first_weight": first_weight, "norm_gain": norm_gain, "norm_bias": norm_bias, "conv_weight": conv_weight, "grad_features": grad_features}


def gelu_slope(values):
    return 0.5 * (1.0 + lax.erf(values * 0.7071067811865476)) + values * jnp.exp(-0.5 * values * values) * 0.3989422804014327

def tap_matrix(hidden, frames_second):
    row_count, frames_first, channels = hidden.shape
    zero_frame = jnp.zeros((row_count, 1, channels), hidden.dtype)
    paired = jnp.concatenate([hidden, zero_frame], axis=1).reshape(row_count, frames_second + 1, 2, channels)
    even_half = paired[:, :, 0]
    odd_half = paired[:, :, 1]
    stacked = jnp.concatenate([even_half[:, :frames_second], odd_half[:, :frames_second], even_half[:, 1:]], axis=2)
    return stacked.reshape(row_count * frames_second, 3 * channels)

def spread_back(back_taps, row_count, frames_second, frames_first):
    first_tap = back_taps[0].reshape(row_count, frames_second, -1)
    middle_tap = back_taps[1].reshape(row_count, frames_second, -1)
    last_tap = back_taps[2].reshape(row_count, frames_second, -1)
    channels = first_tap.shape[2]
    zero_frame = jnp.zeros((row_count, 1, channels), jnp.float32)
    even_half = jnp.concatenate([first_tap, zero_frame], axis=1) + jnp.concatenate([zero_frame, last_tap], axis=1)
    odd_half = jnp.concatenate([middle_tap, zero_frame], axis=1)
    joined = jnp.stack([even_half, odd_half], axis=2).reshape(row_count, 2 * frames_second + 2, channels)
    return joined[:, :frames_first]

def encode_block(wave_rows, row_lengths, first_weight, norm_gain, norm_bias, conv_weight, cotangent):
    row_count, capacity = wave_rows.shape
    channels = norm_gain.shape[0]
    frames_first = capacity // 5 - 1
    frames_second = (capacity // 5 - 2) // 2
    in_length = jnp.arange(capacity)[None, :] < row_lengths[:, None]
    masked = jnp.where(in_length, wave_rows, jnp.zeros_like(wave_rows))
    blocks = masked.reshape(row_count, capacity // 5, 5)
    taps_first = jnp.concatenate([blocks[:, :-1], blocks[:, 1:]], axis=2).reshape(row_count * frames_first, 10)
    conv_first = lax.dot_general(taps_first, first_weight, (((1,), (1,)), ((), ())), preferred_element_type=jnp.float32)
    conv_first = conv_first.reshape(row_count, frames_first, channels)
    count_first = (row_lengths - 10) // 5 + 1
    count_second = (count_first - 3) // 2 + 1
    valid_first = (jnp.arange(frames_first)[None, :] < count_first[:, None]).astype(jnp.float32)[:, :, None]
    valid_second = (jnp.arange(frames_second)[None, :] < count_second[:, None]).astype(jnp.float32)[:, :, None]
    count_float = count_first.astype(jnp.float32)[:, None, None]
    row_mean = lax.optimization_barrier(jnp.sum(conv_first * valid_first, axis=1, keepdims=True)) / count_float
    centred = (conv_first - row_mean) * valid_first
    row_var = lax.optimization_barrier(jnp.sum(centred * centred, axis=1, keepdims=True)) / count_float
    inv_scale = lax.rsqrt(row_var + 1e-05)
    normed = (conv_first - row_mean) * inv_scale
    shifted = normed * norm_gain + norm_bias
    hidden = (jax.nn.gelu(shifted, approximate=False) * valid_first).astype(jnp.bfloat16)
    taps_second = tap_matrix(hidden, frames_second)
    conv_second = lax.dot_general(taps_second, conv_weight, (((1,), (1,)), ((), ())), preferred_element_type=jnp.float32)
    conv_second = conv_second.reshape(row_count, frames_second, channels)
    features = (jax.nn.gelu(conv_second, approximate=False) * valid_second).astype(jnp.bfloat16)
    delta_second = (cotangent.astype(jnp.float32) * valid_second * gelu_slope(conv_second)).astype(jnp.bfloat16)
    delta_flat = delta_second.reshape(row_count * frames_second, channels)
    grad_conv = lax.dot_general(delta_flat, taps_second, (((0,), (0,)), ((), ())), preferred_element_type=jnp.float32)
    back_taps = tuple((jnp.dot(delta_flat, conv_weight[:, tap_index * channels:(tap_index + 1) * channels], preferred_element_type=jnp.float32) for tap_index in range(3)))
    delta_hidden = spread_back(back_taps, row_count, frames_second, frames_first)
    delta_norm = delta_hidden * valid_first * gelu_slope(shifted)
    grad_gain = lax.optimization_barrier(jnp.sum(delta_norm * normed, axis=(0, 1)))
    grad_bias = lax.optimization_barrier(jnp.sum(delta_norm, axis=(0, 1)))
    scaled = delta_norm * norm_gain
    mean_grad = lax.optimization_barrier(jnp.sum(scaled, axis=1, keepdims=True)) / count_float
    mean_cross = lax.optimization_barrier(jnp.sum(scaled * normed, axis=1, keepdims=True)) / count_float
    delta_first = ((scaled - mean_grad - normed * mean_cross) * inv_scale * valid_first).astype(jnp.bfloat16)
    grad_first = lax.dot_general(delta_first.reshape(row_count * frames_first, channels), taps_first, (((0,), (0,)), ((), ())), preferred_element_type=jnp.float32)
    return (features, grad_conv, grad_first, grad_gain, grad_bias)

def reference(waveform, lengths, packing, first_weight, norm_gain, norm_bias, conv_weight, grad_features):
    block_rows = N_GROUP * ROWS_DEV
    wave_blocks = waveform.reshape(N_DP, block_rows, CAP)
    length_blocks = lengths.reshape(N_DP, block_rows)
    pack_blocks = packing.reshape(N_DP, block_rows)
    cot_blocks = grad_features.reshape(N_DP, block_rows, F1, C)

    def block_step(carry, inputs):
        wave_rows, row_lengths, pack_rows, cotangent = inputs
        packed_wave = jnp.zeros_like(wave_rows).at[pack_rows].set(wave_rows)
        packed_lengths = jnp.zeros_like(row_lengths).at[pack_rows].set(row_lengths)
        features, grad_conv, grad_first, grad_gain, grad_bias = encode_block(packed_wave, packed_lengths, first_weight, norm_gain, norm_bias, conv_weight, cotangent)
        return ((carry[0] + grad_conv, carry[1] + grad_first, carry[2] + grad_gain, carry[3] + grad_bias), features)
    start = (jnp.zeros((C, 3 * C), jnp.float32), jnp.zeros((C, 10), jnp.float32), jnp.zeros((C,), jnp.float32), jnp.zeros((C,), jnp.float32))
    totals, features = lax.scan(block_step, start, (wave_blocks, length_blocks, pack_blocks, cot_blocks))
    return (features.reshape(UTTS, F1, C), totals[0], totals[1], totals[2], totals[3])
```

```python
import functools

import jax
import jax.numpy as jnp
from jax import lax
from jax.experimental import pallas as pl
from jax.experimental.pallas import tpu as pltpu
from jax.sharding import PartitionSpec as P

MESH = pl.DeviceIdType.MESH
F32, BF16 = jnp.float32, jnp.bfloat16
STEP = 32


def gelu_slope(values):
    return (
        0.5 * (1.0 + lax.erf(values * 0.7071067811865476))
        + values * jnp.exp(-0.5 * values * values) * 0.3989422804014327
    )


def tap_matrix(hidden, frames_second):
    row_count, frames_first, channels = hidden.shape
    zero_frame = jnp.zeros((row_count, 1, channels), hidden.dtype)
    paired = jnp.concatenate([hidden, zero_frame], axis=1).reshape(
        row_count, frames_second + 1, 2, channels
    )
    even_half = paired[:, :, 0]
    odd_half = paired[:, :, 1]
    stacked = jnp.concatenate(
        [even_half[:, :frames_second], odd_half[:, :frames_second], even_half[:, 1:]], axis=2
    )
    return stacked.reshape(row_count * frames_second, 3 * channels)


def spread_back(back_taps, row_count, frames_second, frames_first):
    first_tap = back_taps[0].reshape(row_count, frames_second, -1)
    middle_tap = back_taps[1].reshape(row_count, frames_second, -1)
    last_tap = back_taps[2].reshape(row_count, frames_second, -1)
    channels = first_tap.shape[2]
    zero_frame = jnp.zeros((row_count, 1, channels), jnp.float32)
    even_half = jnp.concatenate([first_tap, zero_frame], axis=1) + jnp.concatenate(
        [zero_frame, last_tap], axis=1
    )
    odd_half = jnp.concatenate([middle_tap, zero_frame], axis=1)
    joined = jnp.stack([even_half, odd_half], axis=2).reshape(
        row_count, 2 * frames_second + 2, channels
    )
    return joined[:, :frames_first]


def local(
    waveform, lengths, packing, first_weight, norm_gain, norm_bias, conv_weight, grad_features
):
    row_count, capacity = waveform.shape
    channels = norm_gain.shape[0]
    frames_first = capacity // 5 - 1
    frames_second = (capacity // 5 - 2) // 2
    groups = lax.axis_size("group")
    own_group = lax.axis_index("group")
    group_rows = groups * row_count
    all_pack, all_lengths = (
        lax.all_gather(packing, "group", axis=0, tiled=True),
        lax.all_gather(lengths, "group", axis=0, tiled=True),
    )
    target = all_pack // row_count
    slot_index = all_pack % row_count
    positions = jnp.arange(group_rows)
    source = positions // row_count
    same_source = source[:, None] == source[None, :]
    same_target = target[:, None] == target[None, :]
    before = positions[:, None] > positions[None, :]
    rank_among = jnp.sum((same_source & same_target & before).astype(jnp.int32), axis=1)
    arriving = target == own_group
    slot_ids = jnp.arange(row_count)
    choose_slot = (slot_index[None, :] == slot_ids[:, None]) & arriving[None, :]
    local_lengths = jnp.sum(jnp.where(choose_slot, all_lengths[None, :], 0), axis=1)
    per_peer = 2 * ((row_count + 2 * groups - 1) // (2 * groups))
    lane_ids = jnp.arange(per_peer)
    own_target = lax.dynamic_slice_in_dim(target, own_group * row_count, row_count)
    own_rank = lax.dynamic_slice_in_dim(rank_among, own_group * row_count, row_count)
    outgoing = (
        (own_target[None, None, :] == jnp.arange(groups)[:, None, None])
        & (own_rank[None, None, :] == lane_ids[None, :, None])
    ).astype(jnp.bfloat16)
    send_rows = jnp.einsum(
        "gkr,rs->gks", outgoing, waveform, preferred_element_type=jnp.float32
    ).astype(jnp.bfloat16)
    received = lax.all_to_all(send_rows, "group", split_axis=0, concat_axis=0, tiled=True)
    pick_slots = (
        choose_slot[:, :, None] & (rank_among[None, :, None] == lane_ids[None, None, :])
    ).astype(jnp.float32)
    pick_slots = jnp.sum(pick_slots.reshape(row_count, groups, row_count, per_peer), axis=2).astype(
        jnp.bfloat16
    )
    wave_rows = jnp.einsum(
        "lsk,skn->ln", pick_slots, received, preferred_element_type=jnp.float32
    ).astype(jnp.bfloat16)
    first_whole = lax.all_gather(first_weight, "dp", axis=0, tiled=True)
    in_length = jnp.arange(capacity)[None, :] < local_lengths[:, None]
    masked = jnp.where(in_length, wave_rows, jnp.zeros_like(wave_rows))
    blocks = masked.reshape(row_count, capacity // 5, 5)
    taps_first = jnp.concatenate([blocks[:, :-1], blocks[:, 1:]], axis=2).reshape(
        row_count * frames_first, 10
    )
    conv_first = lax.dot_general(
        taps_first, first_whole, (((1,), (1,)), ((), ())), preferred_element_type=jnp.float32
    )
    conv_first = conv_first.reshape(row_count, frames_first, channels)
    count_first = (local_lengths - 10) // 5 + 1
    count_second = (count_first - 3) // 2 + 1
    valid_first = (jnp.arange(frames_first)[None, :] < count_first[:, None]).astype(jnp.float32)[
        :, :, None
    ]
    valid_second = (jnp.arange(frames_second)[None, :] < count_second[:, None]).astype(jnp.float32)[
        :, :, None
    ]
    count_float = count_first.astype(jnp.float32)[:, None, None]
    row_mean = jnp.sum(conv_first * valid_first, axis=1, keepdims=True) / count_float
    centred = (conv_first - row_mean) * valid_first
    row_var = jnp.sum(centred * centred, axis=1, keepdims=True) / count_float
    inv_scale = lax.rsqrt(row_var + 1e-05)
    normed = (conv_first - row_mean) * inv_scale
    shifted = normed * norm_gain + norm_bias
    hidden = (jax.nn.gelu(shifted, approximate=False) * valid_first).astype(jnp.bfloat16)
    taps_second = tap_matrix(hidden, frames_second)
    conv_whole = lax.all_gather(conv_weight, "dp", axis=0, tiled=True)
    conv_second = lax.dot_general(
        taps_second, conv_whole, (((1,), (1,)), ((), ())), preferred_element_type=jnp.float32
    )
    conv_second = conv_second.reshape(row_count, frames_second, channels)
    features = (jax.nn.gelu(conv_second, approximate=False) * valid_second).astype(jnp.bfloat16)
    delta_second = (
        grad_features.astype(jnp.float32) * valid_second * gelu_slope(conv_second)
    ).astype(jnp.bfloat16)
    delta_flat = delta_second.reshape(row_count * frames_second, channels)
    back_taps = tuple(
        (
            jnp.dot(
                delta_flat,
                conv_whole[:, tap_index * channels : (tap_index + 1) * channels],
                preferred_element_type=jnp.float32,
            )
            for tap_index in range(3)
        )
    )
    share = lax.psum_scatter(
        lax.dot_general(
            delta_flat, taps_second, (((0,), (0,)), ((), ())), preferred_element_type=jnp.float32
        ),
        "dp",
        scatter_dimension=0,
        tiled=True,
    )
    grad_conv = lax.psum(share, "group")
    delta_hidden = spread_back(back_taps, row_count, frames_second, frames_first)
    delta_norm = delta_hidden * valid_first * gelu_slope(shifted)
    gain_term = jnp.sum(delta_norm * normed, axis=(0, 1))
    bias_term = jnp.sum(delta_norm, axis=(0, 1))
    scaled = delta_norm * norm_gain
    mean_grad = jnp.sum(scaled, axis=1, keepdims=True) / count_float
    mean_cross = jnp.sum(scaled * normed, axis=1, keepdims=True) / count_float
    delta_first = ((scaled - mean_grad - normed * mean_cross) * inv_scale * valid_first).astype(
        jnp.bfloat16
    )
    first_term = lax.dot_general(
        delta_first.reshape(row_count * frames_first, channels),
        taps_first,
        (((0,), (0,)), ((), ())),
        preferred_element_type=jnp.float32,
    )
    stacked = jnp.concatenate([first_term, gain_term[:, None], bias_term[:, None]], axis=1)
    summed = lax.psum(stacked, ("dp", "group"))
    shard_rows = channels // lax.axis_size("dp")
    grad_first = lax.dynamic_slice_in_dim(
        summed[:, :10], lax.axis_index("dp") * shard_rows, shard_rows, 0
    )
    return (features, grad_conv, grad_first, summed[:, 10], summed[:, 11])


def phi_and_slope(values):
    phi = 0.5 * (1.0 + lax.erf(values * 0.7071067811865476))
    return phi, phi + values * jnp.exp(-0.5 * values * values) * 0.3989422804014327


def fold_rows(block):
    return jnp.sum(block.reshape(block.shape[0] // 8, 8, block.shape[1]), axis=0)


def fused_kernel(
    wave_ref, first_ref, conv_ref, gain_ref, bias_ref, cot_ref,
    feat_ref, gconv_ref, small_ref,
    rows_all, first_all, first_both, conv_all, normed, slope, taps, even_rows, delta, second,
    cot_rows, feat_rows, lhs_all, counts, inv_all, back, dfirst, first_acc, sums,
    gc_full, gc_send, gc_r1, gc_k2, gc_s2, gc_r2, gc_k3, gc_s3, gc_r3, gc_k4, gc_s4, gc_r4, gc_out,
    sm_grp, sm_y, sm_z,
    row_ss, row_rs, first_ss, first_rs, conv_ss, conv_rs, fwd_ss, fwd_rs, own_sem,
    st_ss, st_rs, z_ss, z_rs, out_ss, out_rs, sg_ss, sg_rs, sy_ss, sy_rs, sz_ss, sz_rs,
):
    dp, grp = lax.axis_index("dp"), lax.axis_index("group")
    core, xpos = grp % 2, grp // 2
    ypos, zpos = dp % 2, dp // 2
    partner = (dp, xpos * 2 + (1 - core))
    xpeer = (dp, (1 - xpos) * 2 + core)
    ypeer = (zpos * 2 + (1 - ypos), grp)

    def remote(src, dst, ss, rs, dev):
        return pltpu.make_async_remote_copy(
            src_ref=src, dst_ref=dst, send_sem=ss, recv_sem=rs, device_id=dev, device_id_type=MESH
        )

    barrier = pltpu.get_barrier_semaphore()
    for j in range(1, 4):
        pl.semaphore_signal(barrier, inc=1, device_id=(dp, (grp + j) % 4), device_id_type=MESH)
    for j in range(1, 8):
        pl.semaphore_signal(barrier, inc=1, device_id=((dp + j) % 8, grp), device_id_type=MESH)
    pl.semaphore_wait(barrier, 10)

    row_sends = []
    for j in range(1, 4):
        c = remote(wave_ref, rows_all.at[grp], row_ss.at[j], row_rs.at[grp], (dp, (grp + j) % 4))
        c.start()
        row_sends.append(c)
    first_sends, conv_sends = [], []
    for j in range(1, 8):
        c = remote(first_ref, first_all.at[dp], first_ss.at[j], first_rs.at[dp], ((dp + j) % 8, grp))
        c.start()
        first_sends.append(c)
    for j in range(1, 8):
        c = remote(
            conv_ref.at[core], conv_all.at[dp, core], conv_ss.at[j], conv_rs.at[dp], ((dp + j) % 8, grp)
        )
        c.start()
        conv_sends.append(c)
    own = pltpu.make_async_copy(conv_ref, conv_all.at[dp], own_sem)
    own.start()
    rows_all[grp] = wave_ref[...]
    first_all[dp] = first_ref[...]
    cot_rows[240:256] = jnp.zeros((16, 512), BF16)
    even_rows[256:264] = jnp.zeros((8, 512), F32)
    first_acc[...] = jnp.zeros_like(first_acc)
    sums[...] = jnp.zeros_like(sums)

    for j in range(1, 4):
        p = (grp + j) % 4
        remote(wave_ref, rows_all.at[p], row_ss.at[j], row_rs.at[p], (dp, p)).wait_recv()
    for j in range(1, 8):
        p = (dp + j) % 8
        remote(first_ref, first_all.at[p], first_ss.at[j], first_rs.at[p], (p, grp)).wait_recv()

    for b in range(4):
        joined = first_all[2 * b] + first_all[2 * b + 1]
        lanes = slice(b * 128, b * 128 + 128)
        first_both[0:16, lanes] = joined[0:16]
        first_both[16:32, lanes] = jnp.zeros((16, 128), BF16)
        first_both[:, 512 + b * 128 : 640 + b * 128] = joined[16:48]

    def chunk(i):
        return pl.ds(pl.multiple_of(i * STEP, STEP), STEP)

    def frame_ids(i):
        ids = lax.broadcasted_iota(jnp.int32, (STEP, 512), 0) + i * STEP
        return ids.astype(F32)

    steps = 256 // STEP

    def front(r, _):
        place = (grp * 4 + r).astype(F32)
        chosen = jnp.zeros((16, 256), F32)
        for s in range(4):
            for i in range(4):
                row = rows_all[s, i].astype(F32)
                chosen = chosen + row * (row[10:11] == place).astype(F32)
        lhs_all[r, 0:16] = chosen.astype(BF16)
        lhs_all[r, 16:32] = pltpu.roll(chosen, 255, 1).astype(BF16)
        length = chosen[11:12] * 16.0 + chosen[12:13]
        length = jnp.concatenate([length, length], axis=1)
        count = jnp.floor((length - 9.5) * 0.2) + 1.0
        counts[r] = count
        normed[r] = lax.dot_general(
            lhs_all[r], first_both[...], (((0,), (0,)), ((), ())), preferred_element_type=F32
        )
        inv_count = 1.0 / count

        def add_up(i, acc):
            ids = frame_ids(i) * 2.0
            even = jnp.where(ids < count, normed[r, chunk(i), 0:512], 0.0)
            odd = jnp.where(ids + 1.0 < count, normed[r, chunk(i), 512:1024], 0.0)
            return acc + fold_rows(even + odd)

        total = lax.fori_loop(0, steps, add_up, jnp.zeros((8, 512), F32))
        mean = jnp.sum(total, axis=0, keepdims=True) * inv_count

        def add_squares(i, acc):
            ids = frame_ids(i) * 2.0
            even = jnp.where(ids < count, normed[r, chunk(i), 0:512] - mean, 0.0)
            odd = jnp.where(ids + 1.0 < count, normed[r, chunk(i), 512:1024] - mean, 0.0)
            return acc + fold_rows(even * even + odd * odd)

        total = lax.fori_loop(0, steps, add_squares, jnp.zeros((8, 512), F32))
        inv = lax.rsqrt(jnp.sum(total, axis=0, keepdims=True) * inv_count + 1e-05)
        inv_all[r] = inv
        gain, bias = gain_ref[...], bias_ref[...]

        def activate(i, _):
            ids = frame_ids(i) * 2.0
            rows = pl.ds(pl.multiple_of(r * 256 + i * STEP, STEP), STEP)
            for half in range(2):
                cols = slice(half * 512, half * 512 + 512)
                valid = ids + float(half) < count
                value = (normed[r, chunk(i), cols] - mean) * inv
                normed[r, chunk(i), cols] = value
                shifted = value * gain + bias
                phi, grad = phi_and_slope(shifted)
                hidden = jnp.where(valid, shifted * phi, 0.0)
                slope[r, chunk(i), cols] = jnp.where(valid, grad, 0.0)
                taps[rows, cols] = hidden.astype(BF16)
                if half == 0:
                    even_rows[chunk(i)] = hidden
            return 0

        lax.fori_loop(0, steps, activate, 0)
        all_rows = pl.ds(pl.multiple_of(r * 256, 256), 256)
        taps[all_rows, 1024:1536] = even_rows[1:257].astype(BF16)
        return 0

    lax.fori_loop(0, 4, front, 0)

    forwards = []
    for j in range(1, 8):
        p = (dp + j) % 8
        remote(conv_ref.at[core], conv_all.at[p, core], conv_ss.at[j], conv_rs.at[p], (p, grp)).wait_recv()
        c = remote(conv_all.at[p, core], conv_all.at[p, core], fwd_ss.at[j], fwd_rs.at[p], partner)
        c.start()
        forwards.append(c)
    own.wait()
    for j in range(1, 8):
        p = (dp + j) % 8
        other = conv_all.at[p, 1 - core]
        remote(other, other, fwd_ss.at[j], fwd_rs.at[p], partner).wait_recv()

    def middle(r, _):
        all_rows = pl.ds(pl.multiple_of(r * 256, 256), 256)
        second[...] = lax.dot_general(
            taps[all_rows, :],
            conv_all[...].reshape(512, 1536),
            (((1,), (1,)), ((), ())),
            preferred_element_type=F32,
        )
        cot_rows[0:255] = cot_ref[r]
        count2 = jnp.floor((counts[r] - 2.5) * 0.5) + 1.0

        def activate(i, _):
            valid = frame_ids(i) < count2
            value = second[chunk(i)]
            phi, grad = phi_and_slope(value)
            feat_rows[chunk(i)] = jnp.where(valid, value * phi, 0.0).astype(BF16)
            rows = pl.ds(pl.multiple_of(r * 256 + i * STEP, STEP), STEP)
            delta[rows, :] = jnp.where(valid, cot_rows[chunk(i)].astype(F32) * grad, 0.0).astype(BF16)
            return 0

        lax.fori_loop(0, steps, activate, 0)
        feat_ref[r] = feat_rows[0:255]
        return 0

    lax.fori_loop(0, 4, middle, 0)

    def weight_grad(m, _):
        cols = pl.ds(pl.multiple_of(m * 128, 128), 128)
        part = lax.dot_general(
            delta[:, cols], taps[...], (((0,), (0,)), ((), ())), preferred_element_type=F32
        ).reshape(2, 2, 2, 16, 1536)
        gc_full[pl.ds(m * 2, 2)] = part
        gc_send[pl.ds(m * 2, 2)] = part.astype(BF16)
        return 0

    lax.fori_loop(0, 4, weight_grad, 0)
    stage1 = remote(gc_send.at[:, :, 1 - core], gc_r1, st_ss.at[0], st_rs.at[0], partner)
    stage1.start()

    def backward(r):
        rows = slice(r * 256, r * 256 + 256)
        weights = conv_all[...].reshape(512, 1536)
        part = lax.dot_general(
            delta[rows, :], weights[:, 0:1024], (((1,), (0,)), ((), ())), preferred_element_type=F32
        )
        back[8:264, :] = part
        even_rows[0:8] = jnp.zeros((8, 512), F32)
        even_rows[8:264] = lax.dot_general(
            delta[rows, :], weights[:, 1024:1536], (((1,), (0,)), ((), ())), preferred_element_type=F32
        )
        back[8:264, 0:512] = back[8:264, 0:512] + even_rows[7:263]
        count, inv, gain = counts[r], inv_all[r], gain_ref[...]
        inv_count = 1.0 / count

        def shifted_chunk(i):
            return pl.ds(pl.multiple_of(i * STEP + 8, 8), STEP)

        def norm_sums(i, carry):
            plain, cross = carry
            even = back[shifted_chunk(i), 0:512] * slope[r, chunk(i), 0:512]
            odd = back[shifted_chunk(i), 512:1024] * slope[r, chunk(i), 512:1024]
            back[shifted_chunk(i), 0:512] = even
            back[shifted_chunk(i), 512:1024] = odd
            both = even * normed[r, chunk(i), 0:512] + odd * normed[r, chunk(i), 512:1024]
            return plain + fold_rows(even + odd), cross + fold_rows(both)

        zero = jnp.zeros((8, 512), F32)
        plain, cross = lax.fori_loop(0, steps, norm_sums, (zero, zero))
        plain = jnp.sum(plain, axis=0, keepdims=True)
        cross = jnp.sum(cross, axis=0, keepdims=True)
        sums[0:1] = sums[0:1] + cross
        sums[1:2] = sums[1:2] + plain
        mean_grad = plain * gain * inv_count
        mean_cross = cross * gain * inv_count

        def first_delta(i, _):
            ids = frame_ids(i) * 2.0
            for half in range(2):
                cols = slice(half * 512, half * 512 + 512)
                value = back[shifted_chunk(i), cols] * gain - mean_grad
                value = (value - normed[r, chunk(i), cols] * mean_cross) * inv
                dfirst[chunk(i), cols] = jnp.where(ids + float(half) < count, value, 0.0).astype(BF16)
            return 0

        lax.fori_loop(0, steps, first_delta, 0)
        first_acc[...] += lax.dot_general(
            lhs_all[r], dfirst[...], (((1,), (0,)), ((), ())), preferred_element_type=F32
        )

    backward(0)

    stage1.wait()

    def reduce_core(d, _):
        gc_k2[d] = gc_full[d, xpos, core] + gc_r1[d, xpos].astype(F32)
        gc_s2[d] = (gc_full[d, 1 - xpos, core] + gc_r1[d, 1 - xpos].astype(F32)).astype(BF16)
        return 0

    lax.fori_loop(0, 8, reduce_core, 0)
    stage2 = remote(gc_s2, gc_r2, st_ss.at[1], st_rs.at[1], xpeer)
    stage2.start()

    backward(1)
    backward(2)
    stage2.wait()

    def reduce_x(z, _):
        keep, give = z * 2 + ypos, z * 2 + 1 - ypos
        gc_k3[z] = gc_k2[keep] + gc_r2[keep].astype(F32)
        gc_s3[z] = (gc_k2[give] + gc_r2[give].astype(F32)).astype(BF16)
        return 0

    lax.fori_loop(0, 4, reduce_x, 0)
    stage3 = remote(gc_s3, gc_r3, st_ss.at[2], st_rs.at[2], ypeer)
    stage3.start()

    backward(3)

    small = sm_grp.at[grp]
    small[0:10] = first_acc[0:10, 0:512]
    small[0:5] = small[0:5] + first_acc[5:10, 512:1024]
    small[5:10] = small[5:10] + first_acc[16:21, 512:1024]
    small[10:12] = sums[0:2]
    small[12:16] = jnp.zeros((4, 512), F32)
    sg = []
    for j in range(1, 4):
        c = remote(sm_grp.at[grp], sm_grp.at[grp], sg_ss.at[j], sg_rs.at[grp], (dp, (grp + j) % 4))
        c.start()
        sg.append(c)

    stage3.wait()

    def reduce_y(z, _):
        total = gc_k3[z] + gc_r3[z].astype(F32)
        gc_k4[z] = total
        gc_s4[z] = total.astype(BF16)
        return 0

    lax.fori_loop(0, 4, reduce_y, 0)
    zs = []
    for j in range(1, 4):
        zp = (zpos + j) % 4
        c = remote(gc_s4.at[zp], gc_r4.at[zpos], z_ss.at[j], z_rs.at[zpos], (zp * 2 + ypos, grp))
        c.start()
        zs.append(c)

    for j in range(1, 4):
        p = (grp + j) % 4
        remote(sm_grp.at[p], sm_grp.at[p], sg_ss.at[j], sg_rs.at[p], (dp, p)).wait_recv()
    sm_y[0] = (sm_grp[0] + sm_grp[1]) + (sm_grp[2] + sm_grp[3])
    sy = remote(sm_y.at[0], sm_y.at[1], sy_ss, sy_rs, ypeer)
    sy.start()

    total = gc_k4[zpos]
    for j in range(1, 4):
        zp = (zpos + j) % 4
        remote(gc_s4.at[zp], gc_r4.at[zp], z_ss.at[j], z_rs.at[zp], (zp * 2 + ypos, grp)).wait_recv()
    for j in range(1, 4):
        total = total + gc_r4[(zpos + j) % 4].astype(F32)
    gc_out[grp] = total
    outs = []
    for j in range(1, 4):
        c = remote(gc_out.at[grp], gc_out.at[grp], out_ss.at[j], out_rs.at[grp], (dp, (grp + j) % 4))
        c.start()
        outs.append(c)

    sy.wait()
    sm_z[zpos] = sm_y[0] + sm_y[1]
    sz = []
    for j in range(1, 4):
        zp = (zpos + j) % 4
        c = remote(sm_z.at[zpos], sm_z.at[zpos], sz_ss.at[j], sz_rs.at[zpos], (zp * 2 + ypos, grp))
        c.start()
        sz.append(c)
    for j in range(1, 4):
        p = (grp + j) % 4
        remote(gc_out.at[p], gc_out.at[p], out_ss.at[j], out_rs.at[p], (dp, p)).wait_recv()
    gconv_ref[...] = gc_out[...].reshape(64, 1536)
    for j in range(1, 4):
        zp = (zpos + j) % 4
        remote(sm_z.at[zp], sm_z.at[zp], sz_ss.at[j], sz_rs.at[zp], (zp * 2 + ypos, grp)).wait_recv()
    small_ref[...] = (sm_z[0] + sm_z[1]) + (sm_z[2] + sm_z[3])
    for c in row_sends + first_sends + conv_sends + forwards + sg + zs + outs + sz:
        c.wait_send()


def local_fused(
    waveform, lengths, packing, first_weight, norm_gain, norm_bias, conv_weight, grad_features
):
    dp = lax.axis_index("dp")
    masked = jnp.where(jnp.arange(2560)[None, :] < lengths[:, None], waveform, jnp.zeros_like(waveform))
    blocks = masked.reshape(4, 256, 10).transpose(0, 2, 1)
    notes = jnp.stack([packing, lengths // 16, lengths % 16], axis=1).astype(BF16)
    notes = jnp.broadcast_to(notes[:, :, None], (4, 3, 256))
    wave_rows = jnp.concatenate([blocks, notes, jnp.zeros((4, 3, 256), BF16)], axis=1)
    turned = first_weight.T
    gap = lambda rows: jnp.zeros((rows, 64), BF16)
    stacked = jnp.concatenate(
        [turned, gap(6), gap(5), turned[0:5], gap(6), turned[5:10], gap(11)], axis=0
    )
    odd_half = dp % 2 == 1
    blank = jnp.zeros_like(stacked)
    first_rows = jnp.concatenate(
        [jnp.where(odd_half, blank, stacked), jnp.where(odd_half, stacked, blank)], axis=1
    )
    vmem = lambda *shape: pltpu.VMEM(shape, F32)
    vmem16 = lambda *shape: pltpu.VMEM(shape, BF16)
    dma = pltpu.SemaphoreType.DMA
    features, grad_conv, small = pl.pallas_call(
        fused_kernel,
        out_shape=(
            jax.ShapeDtypeStruct((4, 255, 512), BF16),
            jax.ShapeDtypeStruct((64, 1536), F32),
            jax.ShapeDtypeStruct((16, 512), F32),
        ),
        in_specs=[pl.BlockSpec(memory_space=pltpu.VMEM)] * 6,
        out_specs=[pl.BlockSpec(memory_space=pltpu.VMEM)] * 3,
        scratch_shapes=[
            vmem16(4, 4, 16, 256), vmem16(8, 48, 128), vmem16(32, 1024), vmem16(8, 2, 32, 1536),
            vmem(4, 256, 1024), vmem(4, 256, 1024), vmem16(1024, 1536), vmem(264, 512),
            vmem16(1024, 512), vmem(256, 512),
            vmem16(256, 512), vmem16(256, 512), vmem16(4, 32, 256), vmem(4, 1, 512), vmem(4, 1, 512),
            vmem(264, 1024), vmem16(256, 1024), vmem(32, 1024), vmem(8, 512),
            vmem(8, 2, 2, 16, 1536), vmem16(8, 2, 2, 16, 1536), vmem16(8, 2, 16, 1536),
            vmem(8, 16, 1536), vmem16(8, 16, 1536), vmem16(8, 16, 1536),
            vmem(4, 16, 1536), vmem16(4, 16, 1536), vmem16(4, 16, 1536),
            vmem(4, 16, 1536), vmem16(4, 16, 1536), vmem16(4, 16, 1536), vmem(4, 16, 1536),
            vmem(4, 16, 512), vmem(2, 16, 512), vmem(4, 16, 512),
            dma((4,)), dma((4,)), dma((8,)), dma((8,)), dma((8,)), dma((8,)), dma((8,)), dma((8,)), dma,
            dma((3,)), dma((3,)), dma((4,)), dma((4,)), dma((4,)), dma((4,)), dma((4,)), dma((4,)),
            dma, dma, dma((4,)), dma((4,)),
        ],
        compiler_params=pltpu.CompilerParams(
            collective_id=0, has_side_effects=True, vmem_limit_bytes=60 * 1024 * 1024
        ),
    )(wave_rows, first_rows, conv_weight.reshape(2, 32, 1536), norm_gain[None], norm_bias[None], grad_features)
    grad_first = lax.dynamic_slice_in_dim(small[0:10], dp * 64, 64, 1).T
    return (features, grad_conv, grad_first, small[10], small[11])


def solution(mesh):
    shape = dict(mesh.shape)
    fused = shape["dp"] == 8 and shape["group"] == 4
    return jax.shard_map(
        local_fused if fused else local,
        mesh=mesh,
        in_specs=(
            P(("dp", "group"), None),
            P(("dp", "group")),
            P(("dp", "group")),
            P("dp", None),
            P(),
            P(),
            P("dp", None),
            P(("dp", "group"), None, None),
        ),
        out_specs=(P(("dp", "group"), None, None), P("dp", None), P("dp", None), P(), P()),
        check_vma=False,
    )
```

```python
import functools

import jax
import jax.numpy as jnp
from jax import lax
from jax.experimental import pallas as pl
from jax.experimental.pallas import tpu as pltpu
from jax.sharding import PartitionSpec as P

MESH = pl.DeviceIdType.MESH
F32, BF16 = jnp.float32, jnp.bfloat16
STEP = 32


def gelu_slope(values):
    return (
        0.5 * (1.0 + lax.erf(values * 0.7071067811865476))
        + values * jnp.exp(-0.5 * values * values) * 0.3989422804014327
    )


def tap_matrix(hidden, frames_second):
    row_count, frames_first, channels = hidden.shape
    zero_frame = jnp.zeros((row_count, 1, channels), hidden.dtype)
    paired = jnp.concatenate([hidden, zero_frame], axis=1).reshape(
        row_count, frames_second + 1, 2, channels
    )
    even_half = paired[:, :, 0]
    odd_half = paired[:, :, 1]
    stacked = jnp.concatenate(
        [even_half[:, :frames_second], odd_half[:, :frames_second], even_half[:, 1:]], axis=2
    )
    return stacked.reshape(row_count * frames_second, 3 * channels)


def spread_back(back_taps, row_count, frames_second, frames_first):
    first_tap = back_taps[0].reshape(row_count, frames_second, -1)
    middle_tap = back_taps[1].reshape(row_count, frames_second, -1)
    last_tap = back_taps[2].reshape(row_count, frames_second, -1)
    channels = first_tap.shape[2]
    zero_frame = jnp.zeros((row_count, 1, channels), jnp.float32)
    even_half = jnp.concatenate([first_tap, zero_frame], axis=1) + jnp.concatenate(
        [zero_frame, last_tap], axis=1
    )
    odd_half = jnp.concatenate([middle_tap, zero_frame], axis=1)
    joined = jnp.stack([even_half, odd_half], axis=2).reshape(
        row_count, 2 * frames_second + 2, channels
    )
    return joined[:, :frames_first]


def local(
    waveform, lengths, packing, first_weight, norm_gain, norm_bias, conv_weight, grad_features
):
    row_count, capacity = waveform.shape
    channels = norm_gain.shape[0]
    frames_first = capacity // 5 - 1
    frames_second = (capacity // 5 - 2) // 2
    groups = lax.axis_size("group")
    own_group = lax.axis_index("group")
    group_rows = groups * row_count
    all_pack, all_lengths = (
        lax.all_gather(packing, "group", axis=0, tiled=True),
        lax.all_gather(lengths, "group", axis=0, tiled=True),
    )
    target = all_pack // row_count
    slot_index = all_pack % row_count
    positions = jnp.arange(group_rows)
    source = positions // row_count
    same_source = source[:, None] == source[None, :]
    same_target = target[:, None] == target[None, :]
    before = positions[:, None] > positions[None, :]
    rank_among = jnp.sum((same_source & same_target & before).astype(jnp.int32), axis=1)
    arriving = target == own_group
    slot_ids = jnp.arange(row_count)
    choose_slot = (slot_index[None, :] == slot_ids[:, None]) & arriving[None, :]
    local_lengths = jnp.sum(jnp.where(choose_slot, all_lengths[None, :], 0), axis=1)
    per_peer = 2 * ((row_count + 2 * groups - 1) // (2 * groups))
    lane_ids = jnp.arange(per_peer)
    own_target = lax.dynamic_slice_in_dim(target, own_group * row_count, row_count)
    own_rank = lax.dynamic_slice_in_dim(rank_among, own_group * row_count, row_count)
    outgoing = (
        (own_target[None, None, :] == jnp.arange(groups)[:, None, None])
        & (own_rank[None, None, :] == lane_ids[None, :, None])
    ).astype(jnp.bfloat16)
    send_rows = jnp.einsum(
        "gkr,rs->gks", outgoing, waveform, preferred_element_type=jnp.float32
    ).astype(jnp.bfloat16)
    received = lax.all_to_all(send_rows, "group", split_axis=0, concat_axis=0, tiled=True)
    pick_slots = (
        choose_slot[:, :, None] & (rank_among[None, :, None] == lane_ids[None, None, :])
    ).astype(jnp.float32)
    pick_slots = jnp.sum(pick_slots.reshape(row_count, groups, row_count, per_peer), axis=2).astype(
        jnp.bfloat16
    )
    wave_rows = jnp.einsum(
        "lsk,skn->ln", pick_slots, received, preferred_element_type=jnp.float32
    ).astype(jnp.bfloat16)
    first_whole = lax.all_gather(first_weight, "dp", axis=0, tiled=True)
    in_length = jnp.arange(capacity)[None, :] < local_lengths[:, None]
    masked = jnp.where(in_length, wave_rows, jnp.zeros_like(wave_rows))
    blocks = masked.reshape(row_count, capacity // 5, 5)
    taps_first = jnp.concatenate([blocks[:, :-1], blocks[:, 1:]], axis=2).reshape(
        row_count * frames_first, 10
    )
    conv_first = lax.dot_general(
        taps_first, first_whole, (((1,), (1,)), ((), ())), preferred_element_type=jnp.float32
    )
    conv_first = conv_first.reshape(row_count, frames_first, channels)
    count_first = (local_lengths - 10) // 5 + 1
    count_second = (count_first - 3) // 2 + 1
    valid_first = (jnp.arange(frames_first)[None, :] < count_first[:, None]).astype(jnp.float32)[
        :, :, None
    ]
    valid_second = (jnp.arange(frames_second)[None, :] < count_second[:, None]).astype(jnp.float32)[
        :, :, None
    ]
    count_float = count_first.astype(jnp.float32)[:, None, None]
    row_mean = jnp.sum(conv_first * valid_first, axis=1, keepdims=True) / count_float
    centred = (conv_first - row_mean) * valid_first
    row_var = jnp.sum(centred * centred, axis=1, keepdims=True) / count_float
    inv_scale = lax.rsqrt(row_var + 1e-05)
    normed = (conv_first - row_mean) * inv_scale
    shifted = normed * norm_gain + norm_bias
    hidden = (jax.nn.gelu(shifted, approximate=False) * valid_first).astype(jnp.bfloat16)
    taps_second = tap_matrix(hidden, frames_second)
    conv_whole = lax.all_gather(conv_weight, "dp", axis=0, tiled=True)
    conv_second = lax.dot_general(
        taps_second, conv_whole, (((1,), (1,)), ((), ())), preferred_element_type=jnp.float32
    )
    conv_second = conv_second.reshape(row_count, frames_second, channels)
    features = (jax.nn.gelu(conv_second, approximate=False) * valid_second).astype(jnp.bfloat16)
    delta_second = (
        grad_features.astype(jnp.float32) * valid_second * gelu_slope(conv_second)
    ).astype(jnp.bfloat16)
    delta_flat = delta_second.reshape(row_count * frames_second, channels)
    back_taps = tuple(
        (
            jnp.dot(
                delta_flat,
                conv_whole[:, tap_index * channels : (tap_index + 1) * channels],
                preferred_element_type=jnp.float32,
            )
            for tap_index in range(3)
        )
    )
    share = lax.psum_scatter(
        lax.dot_general(
            delta_flat, taps_second, (((0,), (0,)), ((), ())), preferred_element_type=jnp.float32
        ),
        "dp",
        scatter_dimension=0,
        tiled=True,
    )
    grad_conv = lax.psum(share, "group")
    delta_hidden = spread_back(back_taps, row_count, frames_second, frames_first)
    delta_norm = delta_hidden * valid_first * gelu_slope(shifted)
    gain_term = jnp.sum(delta_norm * normed, axis=(0, 1))
    bias_term = jnp.sum(delta_norm, axis=(0, 1))
    scaled = delta_norm * norm_gain
    mean_grad = jnp.sum(scaled, axis=1, keepdims=True) / count_float
    mean_cross = jnp.sum(scaled * normed, axis=1, keepdims=True) / count_float
    delta_first = ((scaled - mean_grad - normed * mean_cross) * inv_scale * valid_first).astype(
        jnp.bfloat16
    )
    first_term = lax.dot_general(
        delta_first.reshape(row_count * frames_first, channels),
        taps_first,
        (((0,), (0,)), ((), ())),
        preferred_element_type=jnp.float32,
    )
    stacked = jnp.concatenate([first_term, gain_term[:, None], bias_term[:, None]], axis=1)
    summed = lax.psum(stacked, ("dp", "group"))
    shard_rows = channels // lax.axis_size("dp")
    grad_first = lax.dynamic_slice_in_dim(
        summed[:, :10], lax.axis_index("dp") * shard_rows, shard_rows, 0
    )
    return (features, grad_conv, grad_first, summed[:, 10], summed[:, 11])


WIDTH = 384


def phi_and_slope(values):
    phi = 0.5 * (1.0 + lax.erf(values * 0.7071067811865476))
    return phi, phi + values * jnp.exp(-0.5 * values * values) * 0.3989422804014327


def fold_rows(block):
    return jnp.sum(block.reshape(block.shape[0] // 8, 8, block.shape[1]), axis=0)


def fused_kernel(
    wave_ref, first_ref, conv_ref, gain_ref, bias_ref, cot_ref,
    feat_ref, gconv_ref, small_ref,
    rows_all, first_all, first_both, conv_all, normed, slope, taps, even_rows, delta, second,
    cot_rows, feat_rows, lhs_all, counts, inv_all, back, dfirst, first_acc, sums,
    gc_full, gc_send, gc_r1, gc_k2, gc_s2, gc_r2, gc_k3, gc_s3, gc_r3, gc_k4, gc_s4, gc_r4, gc_out,
    sm_grp, sm_y, sm_z,
    row_ss, row_rs, first_ss, first_rs, conv_ss, conv_rs, fwd_ss, fwd_rs, own_sem,
    st_ss, st_rs, z_ss, z_rs, out_ss, out_rs, sg_ss, sg_rs, sy_ss, sy_rs, sz_ss, sz_rs,
):
    dp, grp = lax.axis_index("dp"), lax.axis_index("group")
    core, xpos = grp % 2, grp // 2
    ypos, zpos = dp % 2, dp // 2
    partner = (dp, xpos * 2 + (1 - core))
    xpeer = (dp, (1 - xpos) * 2 + core)
    ypeer = (zpos * 2 + (1 - ypos), grp)

    def remote(src, dst, ss, rs, dev):
        return pltpu.make_async_remote_copy(
            src_ref=src, dst_ref=dst, send_sem=ss, recv_sem=rs, device_id=dev, device_id_type=MESH
        )

    barrier = pltpu.get_barrier_semaphore()
    for j in range(1, 4):
        pl.semaphore_signal(barrier, inc=1, device_id=(dp, (grp + j) % 4), device_id_type=MESH)
    for j in range(1, 8):
        pl.semaphore_signal(barrier, inc=1, device_id=((dp + j) % 8, grp), device_id_type=MESH)
    pl.semaphore_wait(barrier, 10)

    row_sends = []
    for j in range(1, 4):
        c = remote(wave_ref, rows_all.at[grp], row_ss.at[j], row_rs.at[grp], (dp, (grp + j) % 4))
        c.start()
        row_sends.append(c)
    first_sends, conv_sends = [], []
    for j in range(1, 8):
        c = remote(first_ref, first_all.at[dp], first_ss.at[j], first_rs.at[dp], ((dp + j) % 8, grp))
        c.start()
        first_sends.append(c)
    for j in range(1, 4):
        peer = (((zpos + j) % 4) * 2 + ypos, grp)
        c = remote(conv_ref.at[core], conv_all.at[dp, core], conv_ss.at[j], conv_rs.at[dp], peer)
        c.start()
        conv_sends.append(c)
    c = remote(conv_ref.at[core], conv_all.at[dp, core], conv_ss.at[0], conv_rs.at[dp], ypeer)
    c.start()
    conv_sends.append(c)
    own = pltpu.make_async_copy(conv_ref, conv_all.at[dp], own_sem)
    own.start()
    rows_all[grp] = wave_ref[...]
    first_all[dp] = first_ref[...]
    cot_rows[240:256] = jnp.zeros((16, 512), BF16)
    even_rows[256:264] = jnp.zeros((8, 512), F32)
    first_acc[...] = jnp.zeros_like(first_acc)
    sums[...] = jnp.zeros_like(sums)

    for j in range(1, 4):
        p = (grp + j) % 4
        remote(wave_ref, rows_all.at[p], row_ss.at[j], row_rs.at[p], (dp, p)).wait_recv()
    for j in range(1, 8):
        p = (dp + j) % 8
        remote(first_ref, first_all.at[p], first_ss.at[j], first_rs.at[p], (p, grp)).wait_recv()

    for b in range(4):
        joined = first_all[2 * b] + first_all[2 * b + 1]
        lanes = slice(b * 128, b * 128 + 128)
        first_both[0:16, lanes] = joined[0:16]
        first_both[16:32, lanes] = jnp.zeros((16, 128), BF16)
        first_both[:, 512 + b * 128 : 640 + b * 128] = joined[16:48]

    def chunk(i):
        return pl.ds(pl.multiple_of(i * STEP, STEP), STEP)

    def frame_ids(i):
        ids = lax.broadcasted_iota(jnp.int32, (STEP, 512), 0) + i * STEP
        return ids.astype(F32)

    steps = 256 // STEP

    def front(r, _):
        place = (grp * 4 + r).astype(F32)
        chosen = jnp.zeros((16, 256), F32)
        for s in range(4):
            for i in range(4):
                row = rows_all[s, i].astype(F32)
                chosen = chosen + row * (row[10:11] == place).astype(F32)
        lhs_all[r, 0:16] = chosen.astype(BF16)
        lhs_all[r, 16:32] = pltpu.roll(chosen, 255, 1).astype(BF16)
        length = chosen[11:12] * 16.0 + chosen[12:13]
        length = jnp.concatenate([length, length], axis=1)
        count = jnp.floor((length - 9.5) * 0.2) + 1.0
        counts[r] = count
        normed[r] = lax.dot_general(
            lhs_all[r], first_both[...], (((0,), (0,)), ((), ())), preferred_element_type=F32
        )
        inv_count = 1.0 / count

        def add_up(i, acc):
            ids = frame_ids(i) * 2.0
            even = jnp.where(ids < count, normed[r, chunk(i), 0:512], 0.0)
            odd = jnp.where(ids + 1.0 < count, normed[r, chunk(i), 512:1024], 0.0)
            return acc + fold_rows(even + odd)

        total = lax.fori_loop(0, steps, add_up, jnp.zeros((8, 512), F32))
        mean = jnp.sum(total, axis=0, keepdims=True) * inv_count

        def add_squares(i, acc):
            ids = frame_ids(i) * 2.0
            even = jnp.where(ids < count, normed[r, chunk(i), 0:512] - mean, 0.0)
            odd = jnp.where(ids + 1.0 < count, normed[r, chunk(i), 512:1024] - mean, 0.0)
            return acc + fold_rows(even * even + odd * odd)

        total = lax.fori_loop(0, steps, add_squares, jnp.zeros((8, 512), F32))
        inv = lax.rsqrt(jnp.sum(total, axis=0, keepdims=True) * inv_count + 1e-05)
        inv_all[r] = inv
        gain, bias = gain_ref[...], bias_ref[...]

        def activate(i, _):
            ids = frame_ids(i) * 2.0
            rows = pl.ds(pl.multiple_of(r * 256 + i * STEP, STEP), STEP)
            for half in range(2):
                cols = slice(half * 512, half * 512 + 512)
                valid = ids + float(half) < count
                value = (normed[r, chunk(i), cols] - mean) * inv
                normed[r, chunk(i), cols] = value
                shifted = value * gain + bias
                phi, grad = phi_and_slope(shifted)
                hidden = jnp.where(valid, shifted * phi, 0.0)
                slope[r, chunk(i), cols] = jnp.where(valid, grad, 0.0)
                taps[rows, cols] = hidden.astype(BF16)
                if half == 0:
                    even_rows[chunk(i)] = hidden
            return 0

        lax.fori_loop(0, steps, activate, 0)
        all_rows = pl.ds(pl.multiple_of(r * 256, 256), 256)
        taps[all_rows, 1024:1536] = even_rows[1:257].astype(BF16)
        return 0

    lax.fori_loop(0, 2, front, 0)

    forwards = []
    for j in range(1, 4):
        p = ((zpos + j) % 4) * 2 + ypos
        piece = conv_all.at[p, core]
        remote(piece, piece, conv_ss.at[j], conv_rs.at[p], (p, grp)).wait_recv()
        c = remote(piece, piece, conv_ss.at[3 + j], conv_rs.at[p], ypeer)
        c.start()
        forwards.append(c)
        c = remote(piece, piece, fwd_ss.at[j], fwd_rs.at[p], partner)
        c.start()
        forwards.append(c)

    lax.fori_loop(2, 4, front, 0)

    for j in range(4):
        p = ((zpos + j) % 4) * 2 + 1 - ypos
        piece = conv_all.at[p, core]
        remote(piece, piece, conv_ss.at[0], conv_rs.at[p], ypeer).wait_recv()
        c = remote(piece, piece, fwd_ss.at[4 + j], fwd_rs.at[p], partner)
        c.start()
        forwards.append(c)
    own.wait()
    for j in range(1, 8):
        p = (dp + j) % 8
        other = conv_all.at[p, 1 - core]
        remote(other, other, fwd_ss.at[j], fwd_rs.at[p], partner).wait_recv()

    def middle(r, _):
        all_rows = pl.ds(pl.multiple_of(r * 256, 256), 256)
        second[...] = lax.dot_general(
            taps[all_rows, :],
            conv_all[...].reshape(512, 1536),
            (((1,), (1,)), ((), ())),
            preferred_element_type=F32,
        )
        cot_rows[0:255] = cot_ref[r]
        count2 = jnp.floor((counts[r] - 2.5) * 0.5) + 1.0

        def activate(i, _):
            valid = frame_ids(i) < count2
            value = second[chunk(i)]
            phi, grad = phi_and_slope(value)
            feat_rows[chunk(i)] = jnp.where(valid, value * phi, 0.0).astype(BF16)
            rows = pl.ds(pl.multiple_of(r * 256 + i * STEP, STEP), STEP)
            delta[rows, :] = jnp.where(valid, cot_rows[chunk(i)].astype(F32) * grad, 0.0).astype(BF16)
            return 0

        lax.fori_loop(0, steps, activate, 0)
        feat_ref[r] = feat_rows[0:255]
        return 0

    lax.fori_loop(0, 4, middle, 0)

    stage = {}

    def weight_grad(b):
        def rows_of(m, _):
            cols = pl.ds(pl.multiple_of(m * 128, 128), 128)
            part = lax.dot_general(
                delta[:, cols],
                taps[:, b * WIDTH : (b + 1) * WIDTH],
                (((0,), (0,)), ((), ())),
                preferred_element_type=F32,
            ).reshape(2, 2, 2, 16, WIDTH)
            gc_full[b, pl.ds(m * 2, 2)] = part
            gc_send[b, pl.ds(m * 2, 2)] = part.astype(BF16)
            return 0

        lax.fori_loop(0, 4, rows_of, 0)
        stage[b, 0] = remote(gc_send.at[b, :, :, 1 - core], gc_r1.at[b], st_ss.at[b, 0], st_rs.at[b, 0], partner)
        stage[b, 0].start()

    def reduce_first(b):
        stage[b, 0].wait()

        def one(i, _):
            if b % 2 == 0:
                keep, give = (i, xpos), (i, 1 - xpos)
            else:
                keep, give = ((i // 2) * 2 + ypos, i % 2), ((i // 2) * 2 + 1 - ypos, i % 2)
            gc_k2[b, i] = gc_full[b, keep[0], keep[1], core] + gc_r1[b, keep[0], keep[1]].astype(F32)
            gc_s2[b, i] = (
                gc_full[b, give[0], give[1], core] + gc_r1[b, give[0], give[1]].astype(F32)
            ).astype(BF16)
            return 0

        lax.fori_loop(0, 8, one, 0)
        peer = xpeer if b % 2 == 0 else ypeer
        stage[b, 1] = remote(gc_s2.at[b], gc_r2.at[b], st_ss.at[b, 1], st_rs.at[b, 1], peer)
        stage[b, 1].start()

    def reduce_second(b):
        stage[b, 1].wait()
        place = ypos if b % 2 == 0 else xpos

        def one(z, _):
            keep, give = z * 2 + place, z * 2 + 1 - place
            gc_k3[b, z] = gc_k2[b, keep] + gc_r2[b, keep].astype(F32)
            gc_s3[b, z] = (gc_k2[b, give] + gc_r2[b, give].astype(F32)).astype(BF16)
            return 0

        lax.fori_loop(0, 4, one, 0)
        peer = ypeer if b % 2 == 0 else xpeer
        stage[b, 2] = remote(gc_s3.at[b], gc_r3.at[b], st_ss.at[b, 2], st_rs.at[b, 2], peer)
        stage[b, 2].start()

    late_sends = []

    def reduce_third(b):
        stage[b, 2].wait()

        def one(z, _):
            total = gc_k3[b, z] + gc_r3[b, z].astype(F32)
            gc_k4[b, z] = total
            gc_s4[b, z] = total.astype(BF16)
            return 0

        lax.fori_loop(0, 4, one, 0)
        for j in range(1, 4):
            zp = (zpos + j) % 4
            c = remote(
                gc_s4.at[b, zp], gc_r4.at[b, zpos], z_ss.at[b, j], z_rs.at[b, zpos], (zp * 2 + ypos, grp)
            )
            c.start()
            late_sends.append(c)

    def reduce_last(b):
        total = gc_k4[b, zpos]
        for j in range(1, 4):
            zp = (zpos + j) % 4
            piece = gc_r4.at[b, zp]
            remote(piece, piece, z_ss.at[b, j], z_rs.at[b, zp], (zp * 2 + ypos, grp)).wait_recv()
            total = total + gc_r4[b, zp].astype(F32)
        gc_out[b, grp] = total.astype(BF16)
        for j in range(1, 4):
            c = remote(
                gc_out.at[b, grp], gc_out.at[b, grp], out_ss.at[b, j], out_rs.at[b, grp], (dp, (grp + j) % 4)
            )
            c.start()
            late_sends.append(c)

    def gathered(b):
        for j in range(1, 4):
            p = (grp + j) % 4
            piece = gc_out.at[b, p]
            remote(piece, piece, out_ss.at[b, j], out_rs.at[b, p], (dp, p)).wait_recv()
        gconv_ref[:, b * WIDTH : (b + 1) * WIDTH] = gc_out[b].astype(F32).reshape(64, WIDTH)

    def backward(r):
        rows = slice(r * 256, r * 256 + 256)
        weights = conv_all[...].reshape(512, 1536)
        part = lax.dot_general(
            delta[rows, :], weights[:, 0:1024], (((1,), (0,)), ((), ())), preferred_element_type=F32
        )
        back[8:264, :] = part
        even_rows[0:8] = jnp.zeros((8, 512), F32)
        even_rows[8:264] = lax.dot_general(
            delta[rows, :], weights[:, 1024:1536], (((1,), (0,)), ((), ())), preferred_element_type=F32
        )
        back[8:264, 0:512] = back[8:264, 0:512] + even_rows[7:263]
        count, inv, gain = counts[r], inv_all[r], gain_ref[...]
        inv_count = 1.0 / count

        def shifted_chunk(i):
            return pl.ds(pl.multiple_of(i * STEP + 8, 8), STEP)

        def norm_sums(i, carry):
            plain, cross = carry
            even = back[shifted_chunk(i), 0:512] * slope[r, chunk(i), 0:512]
            odd = back[shifted_chunk(i), 512:1024] * slope[r, chunk(i), 512:1024]
            back[shifted_chunk(i), 0:512] = even
            back[shifted_chunk(i), 512:1024] = odd
            both = even * normed[r, chunk(i), 0:512] + odd * normed[r, chunk(i), 512:1024]
            return plain + fold_rows(even + odd), cross + fold_rows(both)

        zero = jnp.zeros((8, 512), F32)
        plain, cross = lax.fori_loop(0, steps, norm_sums, (zero, zero))
        plain = jnp.sum(plain, axis=0, keepdims=True)
        cross = jnp.sum(cross, axis=0, keepdims=True)
        sums[0:1] = sums[0:1] + cross
        sums[1:2] = sums[1:2] + plain
        mean_grad = plain * gain * inv_count
        mean_cross = cross * gain * inv_count

        def first_delta(i, _):
            ids = frame_ids(i) * 2.0
            for half in range(2):
                cols = slice(half * 512, half * 512 + 512)
                value = back[shifted_chunk(i), cols] * gain - mean_grad
                value = (value - normed[r, chunk(i), cols] * mean_cross) * inv
                dfirst[chunk(i), cols] = jnp.where(ids + float(half) < count, value, 0.0).astype(BF16)
            return 0

        lax.fori_loop(0, steps, first_delta, 0)
        first_acc[...] += lax.dot_general(
            lhs_all[r], dfirst[...], (((1,), (0,)), ((), ())), preferred_element_type=F32
        )

    weight_grad(0)
    weight_grad(1)
    weight_grad(2)
    weight_grad(3)
    reduce_first(0)
    reduce_first(1)
    backward(0)
    reduce_first(2)
    reduce_first(3)
    backward(1)
    backward(2)
    reduce_second(0)
    reduce_second(1)
    backward(3)

    small = sm_grp.at[grp]
    small[0:10] = first_acc[0:10, 0:512]
    small[0:5] = small[0:5] + first_acc[5:10, 512:1024]
    small[5:10] = small[5:10] + first_acc[16:21, 512:1024]
    small[10:12] = sums[0:2]
    small[12:16] = jnp.zeros((4, 512), F32)
    for j in range(1, 4):
        c = remote(sm_grp.at[grp], sm_grp.at[grp], sg_ss.at[j], sg_rs.at[grp], (dp, (grp + j) % 4))
        c.start()
        late_sends.append(c)

    reduce_third(0)
    reduce_third(1)

    for j in range(1, 4):
        p = (grp + j) % 4
        remote(sm_grp.at[p], sm_grp.at[p], sg_ss.at[j], sg_rs.at[p], (dp, p)).wait_recv()
    sm_y[0] = (sm_grp[0] + sm_grp[1]) + (sm_grp[2] + sm_grp[3])
    sy = remote(sm_y.at[0], sm_y.at[1], sy_ss, sy_rs, ypeer)
    sy.start()

    reduce_second(2)
    reduce_second(3)
    sy.wait()
    sm_z[zpos] = sm_y[0] + sm_y[1]
    for j in range(1, 4):
        zp = (zpos + j) % 4
        c = remote(sm_z.at[zpos], sm_z.at[zpos], sz_ss.at[j], sz_rs.at[zpos], (zp * 2 + ypos, grp))
        c.start()
        late_sends.append(c)
    reduce_third(2)
    reduce_third(3)
    for b in range(4):
        reduce_last(b)
    for j in range(1, 4):
        zp = (zpos + j) % 4
        remote(sm_z.at[zp], sm_z.at[zp], sz_ss.at[j], sz_rs.at[zp], (zp * 2 + ypos, grp)).wait_recv()
    small_ref[...] = (sm_z[0] + sm_z[1]) + (sm_z[2] + sm_z[3])
    for b in range(4):
        gathered(b)
    for c in row_sends + first_sends + conv_sends + forwards + late_sends:
        c.wait_send()


def local_fused(
    waveform, lengths, packing, first_weight, norm_gain, norm_bias, conv_weight, grad_features
):
    dp = lax.axis_index("dp")
    masked = jnp.where(jnp.arange(2560)[None, :] < lengths[:, None], waveform, jnp.zeros_like(waveform))
    blocks = masked.reshape(4, 256, 10).transpose(0, 2, 1)
    notes = jnp.stack([packing, lengths // 16, lengths % 16], axis=1).astype(BF16)
    notes = jnp.broadcast_to(notes[:, :, None], (4, 3, 256))
    wave_rows = jnp.concatenate([blocks, notes, jnp.zeros((4, 3, 256), BF16)], axis=1)
    turned = first_weight.T
    gap = lambda rows: jnp.zeros((rows, 64), BF16)
    stacked = jnp.concatenate(
        [turned, gap(6), gap(5), turned[0:5], gap(6), turned[5:10], gap(11)], axis=0
    )
    odd_half = dp % 2 == 1
    blank = jnp.zeros_like(stacked)
    first_rows = jnp.concatenate(
        [jnp.where(odd_half, blank, stacked), jnp.where(odd_half, stacked, blank)], axis=1
    )
    vmem = lambda *shape: pltpu.VMEM(shape, F32)
    vmem16 = lambda *shape: pltpu.VMEM(shape, BF16)
    dma = pltpu.SemaphoreType.DMA
    features, grad_conv, small = pl.pallas_call(
        fused_kernel,
        out_shape=(
            jax.ShapeDtypeStruct((4, 255, 512), BF16),
            jax.ShapeDtypeStruct((64, 1536), F32),
            jax.ShapeDtypeStruct((16, 512), F32),
        ),
        in_specs=[pl.BlockSpec(memory_space=pltpu.VMEM)] * 6,
        out_specs=[pl.BlockSpec(memory_space=pltpu.VMEM)] * 3,
        scratch_shapes=[
            vmem16(4, 4, 16, 256), vmem16(8, 48, 128), vmem16(32, 1024), vmem16(8, 2, 32, 1536),
            vmem(4, 256, 1024), vmem(4, 256, 1024), vmem16(1024, 1536), vmem(264, 512),
            vmem16(1024, 512), vmem(256, 512),
            vmem16(256, 512), vmem16(256, 512), vmem16(4, 32, 256), vmem(4, 1, 512), vmem(4, 1, 512),
            vmem(264, 1024), vmem16(256, 1024), vmem(32, 1024), vmem(8, 512),
            vmem(4, 8, 2, 2, 16, WIDTH), vmem16(4, 8, 2, 2, 16, WIDTH), vmem16(4, 8, 2, 16, WIDTH),
            vmem(4, 8, 16, WIDTH), vmem16(4, 8, 16, WIDTH), vmem16(4, 8, 16, WIDTH),
            vmem(4, 4, 16, WIDTH), vmem16(4, 4, 16, WIDTH), vmem16(4, 4, 16, WIDTH),
            vmem(4, 4, 16, WIDTH), vmem16(4, 4, 16, WIDTH), vmem16(4, 4, 16, WIDTH),
            vmem16(4, 4, 16, WIDTH),
            vmem(4, 16, 512), vmem(2, 16, 512), vmem(4, 16, 512),
            dma((4,)), dma((4,)), dma((8,)), dma((8,)), dma((8,)), dma((8,)), dma((8,)), dma((8,)), dma,
            dma((4, 3)), dma((4, 3)), dma((4, 4)), dma((4, 4)), dma((4, 4)), dma((4, 4)), dma((4,)), dma((4,)),
            dma, dma, dma((4,)), dma((4,)),
        ],
        compiler_params=pltpu.CompilerParams(
            collective_id=0, has_side_effects=True, vmem_limit_bytes=60 * 1024 * 1024
        ),
    )(wave_rows, first_rows, conv_weight.reshape(2, 32, 1536), norm_gain[None], norm_bias[None], grad_features)
    grad_first = lax.dynamic_slice_in_dim(small[0:10], dp * 64, 64, 1).T
    return (features, grad_conv, grad_first, small[10], small[11])


def solution(mesh):
    shape = dict(mesh.shape)
    fused = shape["dp"] == 8 and shape["group"] == 4
    return jax.shard_map(
        local_fused if fused else local,
        mesh=mesh,
        in_specs=(
            P(("dp", "group"), None),
            P(("dp", "group")),
            P(("dp", "group")),
            P("dp", None),
            P(),
            P(),
            P("dp", None),
            P(("dp", "group"), None, None),
        ),
        out_specs=(P(("dp", "group"), None, None), P("dp", None), P("dp", None), P(), P()),
        check_vma=False,
    )
```

```python
import functools

import jax
import jax.numpy as jnp
from jax import lax
from jax.experimental import pallas as pl
from jax.experimental.pallas import tpu as pltpu
from jax.sharding import PartitionSpec as P

MESH = pl.DeviceIdType.MESH
F32, BF16 = jnp.float32, jnp.bfloat16
STEP = 32


def gelu_slope(values):
    return (
        0.5 * (1.0 + lax.erf(values * 0.7071067811865476))
        + values * jnp.exp(-0.5 * values * values) * 0.3989422804014327
    )


def tap_matrix(hidden, frames_second):
    row_count, frames_first, channels = hidden.shape
    zero_frame = jnp.zeros((row_count, 1, channels), hidden.dtype)
    paired = jnp.concatenate([hidden, zero_frame], axis=1).reshape(
        row_count, frames_second + 1, 2, channels
    )
    even_half = paired[:, :, 0]
    odd_half = paired[:, :, 1]
    stacked = jnp.concatenate(
        [even_half[:, :frames_second], odd_half[:, :frames_second], even_half[:, 1:]], axis=2
    )
    return stacked.reshape(row_count * frames_second, 3 * channels)


def spread_back(back_taps, row_count, frames_second, frames_first):
    first_tap = back_taps[0].reshape(row_count, frames_second, -1)
    middle_tap = back_taps[1].reshape(row_count, frames_second, -1)
    last_tap = back_taps[2].reshape(row_count, frames_second, -1)
    channels = first_tap.shape[2]
    zero_frame = jnp.zeros((row_count, 1, channels), jnp.float32)
    even_half = jnp.concatenate([first_tap, zero_frame], axis=1) + jnp.concatenate(
        [zero_frame, last_tap], axis=1
    )
    odd_half = jnp.concatenate([middle_tap, zero_frame], axis=1)
    joined = jnp.stack([even_half, odd_half], axis=2).reshape(
        row_count, 2 * frames_second + 2, channels
    )
    return joined[:, :frames_first]


def local(
    waveform, lengths, packing, first_weight, norm_gain, norm_bias, conv_weight, grad_features
):
    row_count, capacity = waveform.shape
    channels = norm_gain.shape[0]
    frames_first = capacity // 5 - 1
    frames_second = (capacity // 5 - 2) // 2
    groups = lax.axis_size("group")
    own_group = lax.axis_index("group")
    group_rows = groups * row_count
    all_pack, all_lengths = (
        lax.all_gather(packing, "group", axis=0, tiled=True),
        lax.all_gather(lengths, "group", axis=0, tiled=True),
    )
    target = all_pack // row_count
    slot_index = all_pack % row_count
    positions = jnp.arange(group_rows)
    source = positions // row_count
    same_source = source[:, None] == source[None, :]
    same_target = target[:, None] == target[None, :]
    before = positions[:, None] > positions[None, :]
    rank_among = jnp.sum((same_source & same_target & before).astype(jnp.int32), axis=1)
    arriving = target == own_group
    slot_ids = jnp.arange(row_count)
    choose_slot = (slot_index[None, :] == slot_ids[:, None]) & arriving[None, :]
    local_lengths = jnp.sum(jnp.where(choose_slot, all_lengths[None, :], 0), axis=1)
    per_peer = 2 * ((row_count + 2 * groups - 1) // (2 * groups))
    lane_ids = jnp.arange(per_peer)
    own_target = lax.dynamic_slice_in_dim(target, own_group * row_count, row_count)
    own_rank = lax.dynamic_slice_in_dim(rank_among, own_group * row_count, row_count)
    outgoing = (
        (own_target[None, None, :] == jnp.arange(groups)[:, None, None])
        & (own_rank[None, None, :] == lane_ids[None, :, None])
    ).astype(jnp.bfloat16)
    send_rows = jnp.einsum(
        "gkr,rs->gks", outgoing, waveform, preferred_element_type=jnp.float32
    ).astype(jnp.bfloat16)
    received = lax.all_to_all(send_rows, "group", split_axis=0, concat_axis=0, tiled=True)
    pick_slots = (
        choose_slot[:, :, None] & (rank_among[None, :, None] == lane_ids[None, None, :])
    ).astype(jnp.float32)
    pick_slots = jnp.sum(pick_slots.reshape(row_count, groups, row_count, per_peer), axis=2).astype(
        jnp.bfloat16
    )
    wave_rows = jnp.einsum(
        "lsk,skn->ln", pick_slots, received, preferred_element_type=jnp.float32
    ).astype(jnp.bfloat16)
    first_whole = lax.all_gather(first_weight, "dp", axis=0, tiled=True)
    in_length = jnp.arange(capacity)[None, :] < local_lengths[:, None]
    masked = jnp.where(in_length, wave_rows, jnp.zeros_like(wave_rows))
    blocks = masked.reshape(row_count, capacity // 5, 5)
    taps_first = jnp.concatenate([blocks[:, :-1], blocks[:, 1:]], axis=2).reshape(
        row_count * frames_first, 10
    )
    conv_first = lax.dot_general(
        taps_first, first_whole, (((1,), (1,)), ((), ())), preferred_element_type=jnp.float32
    )
    conv_first = conv_first.reshape(row_count, frames_first, channels)
    count_first = (local_lengths - 10) // 5 + 1
    count_second = (count_first - 3) // 2 + 1
    valid_first = (jnp.arange(frames_first)[None, :] < count_first[:, None]).astype(jnp.float32)[
        :, :, None
    ]
    valid_second = (jnp.arange(frames_second)[None, :] < count_second[:, None]).astype(jnp.float32)[
        :, :, None
    ]
    count_float = count_first.astype(jnp.float32)[:, None, None]
    row_mean = jnp.sum(conv_first * valid_first, axis=1, keepdims=True) / count_float
    centred = (conv_first - row_mean) * valid_first
    row_var = jnp.sum(centred * centred, axis=1, keepdims=True) / count_float
    inv_scale = lax.rsqrt(row_var + 1e-05)
    normed = (conv_first - row_mean) * inv_scale
    shifted = normed * norm_gain + norm_bias
    hidden = (jax.nn.gelu(shifted, approximate=False) * valid_first).astype(jnp.bfloat16)
    taps_second = tap_matrix(hidden, frames_second)
    conv_whole = lax.all_gather(conv_weight, "dp", axis=0, tiled=True)
    conv_second = lax.dot_general(
        taps_second, conv_whole, (((1,), (1,)), ((), ())), preferred_element_type=jnp.float32
    )
    conv_second = conv_second.reshape(row_count, frames_second, channels)
    features = (jax.nn.gelu(conv_second, approximate=False) * valid_second).astype(jnp.bfloat16)
    delta_second = (
        grad_features.astype(jnp.float32) * valid_second * gelu_slope(conv_second)
    ).astype(jnp.bfloat16)
    delta_flat = delta_second.reshape(row_count * frames_second, channels)
    back_taps = tuple(
        (
            jnp.dot(
                delta_flat,
                conv_whole[:, tap_index * channels : (tap_index + 1) * channels],
                preferred_element_type=jnp.float32,
            )
            for tap_index in range(3)
        )
    )
    share = lax.psum_scatter(
        lax.dot_general(
            delta_flat, taps_second, (((0,), (0,)), ((), ())), preferred_element_type=jnp.float32
        ),
        "dp",
        scatter_dimension=0,
        tiled=True,
    )
    grad_conv = lax.psum(share, "group")
    delta_hidden = spread_back(back_taps, row_count, frames_second, frames_first)
    delta_norm = delta_hidden * valid_first * gelu_slope(shifted)
    gain_term = jnp.sum(delta_norm * normed, axis=(0, 1))
    bias_term = jnp.sum(delta_norm, axis=(0, 1))
    scaled = delta_norm * norm_gain
    mean_grad = jnp.sum(scaled, axis=1, keepdims=True) / count_float
    mean_cross = jnp.sum(scaled * normed, axis=1, keepdims=True) / count_float
    delta_first = ((scaled - mean_grad - normed * mean_cross) * inv_scale * valid_first).astype(
        jnp.bfloat16
    )
    first_term = lax.dot_general(
        delta_first.reshape(row_count * frames_first, channels),
        taps_first,
        (((0,), (0,)), ((), ())),
        preferred_element_type=jnp.float32,
    )
    stacked = jnp.concatenate([first_term, gain_term[:, None], bias_term[:, None]], axis=1)
    summed = lax.psum(stacked, ("dp", "group"))
    shard_rows = channels // lax.axis_size("dp")
    grad_first = lax.dynamic_slice_in_dim(
        summed[:, :10], lax.axis_index("dp") * shard_rows, shard_rows, 0
    )
    return (features, grad_conv, grad_first, summed[:, 10], summed[:, 11])


WIDTH = 384


def phi_and_slope(values):
    phi = 0.5 * (1.0 + lax.erf(values * 0.7071067811865476))
    return phi, phi + values * jnp.exp(-0.5 * values * values) * 0.3989422804014327


def fold_rows(block):
    return jnp.sum(block.reshape(block.shape[0] // 8, 8, block.shape[1]), axis=0)


def fused_kernel(
    wave_ref, first_ref, conv_ref, gain_ref, bias_ref, cot_ref,
    feat_ref, gconv_ref, gfirst_ref, ggain_ref, gbias_ref,
    rows_all, first_all, first_both, conv_all, normed, slope, taps, even_rows, delta, second,
    cot_wide, cot_rows, feat_wide, feat_rows, lhs_all, counts, inv_all, back, dfirst, first_acc, sums,
    gc_full, gc_send, gc_r1, gc_k2, gc_s2, gc_r2, gc_k3, gc_s3, gc_r3, gc_k4, gc_s4, gc_r4, gc_out,
    sm_grp, sm_y, sm_z,
    row_ss, row_rs, first_ss, first_rs, conv_ss, conv_rs, fwd_ss, fwd_rs, own_sem, cot_sem, feat_sem,
    st_ss, st_rs, z_ss, z_rs, out_ss, out_rs, sg_ss, sg_rs, sy_ss, sy_rs, sz_ss, sz_rs,
):
    dp, grp = lax.axis_index("dp"), lax.axis_index("group")
    core, xpos = grp % 2, grp // 2
    ypos, zpos = dp % 2, dp // 2
    partner = (dp, xpos * 2 + (1 - core))
    xpeer = (dp, (1 - xpos) * 2 + core)
    ypeer = (zpos * 2 + (1 - ypos), grp)

    def chunk(i):
        return pl.ds(pl.multiple_of(i * STEP, STEP), STEP)

    def frame_ids(i):
        ids = lax.broadcasted_iota(jnp.int32, (STEP, 512), 0) + i * STEP
        return ids.astype(F32)

    steps = 256 // STEP

    def remote(src, dst, ss, rs, dev):
        return pltpu.make_async_remote_copy(
            src_ref=src, dst_ref=dst, send_sem=ss, recv_sem=rs, device_id=dev, device_id_type=MESH
        )

    cot_in = pltpu.make_async_copy(cot_ref, cot_wide.at[0:255], cot_sem)
    cot_in.start()
    barrier = pltpu.get_barrier_semaphore()
    for j in range(1, 4):
        pl.semaphore_signal(barrier, inc=1, device_id=(dp, (grp + j) % 4), device_id_type=MESH)
    for j in range(1, 8):
        pl.semaphore_signal(barrier, inc=1, device_id=((dp + j) % 8, grp), device_id_type=MESH)
    cot_wide[255] = jnp.zeros((4, 512), BF16)
    even_rows[256:264] = jnp.zeros((8, 512), F32)
    first_acc[...] = jnp.zeros_like(first_acc)
    sums[...] = jnp.zeros_like(sums)
    cot_in.wait()

    def split_rows(i, _):
        block = cot_wide[chunk(i)].astype(F32)
        for r in range(4):
            cot_rows[r, chunk(i)] = block[:, r, :].astype(BF16)
        return 0

    lax.fori_loop(0, steps, split_rows, 0)
    pl.semaphore_wait(barrier, 10)

    row_sends = []
    for j in range(1, 4):
        c = remote(wave_ref, rows_all.at[grp], row_ss.at[j], row_rs.at[grp], (dp, (grp + j) % 4))
        c.start()
        row_sends.append(c)
    first_sends, conv_sends = [], []
    for j in range(1, 8):
        c = remote(first_ref, first_all.at[dp], first_ss.at[j], first_rs.at[dp], ((dp + j) % 8, grp))
        c.start()
        first_sends.append(c)
    for j in range(1, 4):
        peer = (((zpos + j) % 4) * 2 + ypos, grp)
        c = remote(conv_ref.at[core], conv_all.at[dp, core], conv_ss.at[j], conv_rs.at[dp], peer)
        c.start()
        conv_sends.append(c)
    c = remote(conv_ref.at[core], conv_all.at[dp, core], conv_ss.at[0], conv_rs.at[dp], ypeer)
    c.start()
    conv_sends.append(c)
    own = pltpu.make_async_copy(conv_ref, conv_all.at[dp], own_sem)
    own.start()
    rows_all[grp] = wave_ref[...]
    first_all[dp] = first_ref[...]

    for j in range(1, 4):
        p = (grp + j) % 4
        remote(wave_ref, rows_all.at[p], row_ss.at[j], row_rs.at[p], (dp, p)).wait_recv()
    for j in range(1, 8):
        p = (dp + j) % 8
        remote(first_ref, first_all.at[p], first_ss.at[j], first_rs.at[p], (p, grp)).wait_recv()

    for b in range(4):
        joined = first_all[2 * b] + first_all[2 * b + 1]
        lanes = slice(b * 128, b * 128 + 128)
        first_both[0:16, lanes] = joined[0:16]
        first_both[16:32, lanes] = jnp.zeros((16, 128), BF16)
        first_both[:, 512 + b * 128 : 640 + b * 128] = joined[16:48]

    def front(r, _):
        place = (grp * 4 + r).astype(F32)
        chosen = jnp.zeros((16, 256), F32)
        for s in range(4):
            for i in range(4):
                row = rows_all[s, i].astype(F32)
                chosen = chosen + row * (row[10:11] == place).astype(F32)
        lhs_all[r, 0:16] = chosen.astype(BF16)
        lhs_all[r, 16:32] = pltpu.roll(chosen, 255, 1).astype(BF16)
        length = chosen[11:12] * 16.0 + chosen[12:13]
        length = jnp.concatenate([length, length], axis=1)
        count = jnp.floor((length - 9.5) * 0.2) + 1.0
        counts[r] = count
        normed[r] = lax.dot_general(
            lhs_all[r], first_both[...], (((0,), (0,)), ((), ())), preferred_element_type=F32
        )
        inv_count = 1.0 / count

        def add_up(i, acc):
            ids = frame_ids(i) * 2.0
            even = jnp.where(ids < count, normed[r, chunk(i), 0:512], 0.0)
            odd = jnp.where(ids + 1.0 < count, normed[r, chunk(i), 512:1024], 0.0)
            return acc + fold_rows(even + odd)

        total = lax.fori_loop(0, steps, add_up, jnp.zeros((8, 512), F32))
        mean = jnp.sum(total, axis=0, keepdims=True) * inv_count

        def add_squares(i, acc):
            ids = frame_ids(i) * 2.0
            even = jnp.where(ids < count, normed[r, chunk(i), 0:512] - mean, 0.0)
            odd = jnp.where(ids + 1.0 < count, normed[r, chunk(i), 512:1024] - mean, 0.0)
            return acc + fold_rows(even * even + odd * odd)

        total = lax.fori_loop(0, steps, add_squares, jnp.zeros((8, 512), F32))
        inv = lax.rsqrt(jnp.sum(total, axis=0, keepdims=True) * inv_count + 1e-05)
        inv_all[r] = inv
        gain, bias = gain_ref[...], bias_ref[...]

        def activate(i, _):
            ids = frame_ids(i) * 2.0
            rows = pl.ds(pl.multiple_of(r * 256 + i * STEP, STEP), STEP)
            for half in range(2):
                cols = slice(half * 512, half * 512 + 512)
                valid = ids + float(half) < count
                value = (normed[r, chunk(i), cols] - mean) * inv
                normed[r, chunk(i), cols] = value
                shifted = value * gain + bias
                phi, grad = phi_and_slope(shifted)
                hidden = jnp.where(valid, shifted * phi, 0.0)
                slope[r, chunk(i), cols] = jnp.where(valid, grad, 0.0)
                taps[rows, cols] = hidden.astype(BF16)
                if half == 0:
                    even_rows[chunk(i)] = hidden
            return 0

        lax.fori_loop(0, steps, activate, 0)
        all_rows = pl.ds(pl.multiple_of(r * 256, 256), 256)
        taps[all_rows, 1024:1536] = even_rows[1:257].astype(BF16)
        return 0

    lax.fori_loop(0, 2, front, 0)

    forwards = []
    for j in range(1, 4):
        p = ((zpos + j) % 4) * 2 + ypos
        piece = conv_all.at[p, core]
        remote(piece, piece, conv_ss.at[j], conv_rs.at[p], (p, grp)).wait_recv()
        c = remote(piece, piece, conv_ss.at[3 + j], conv_rs.at[p], ypeer)
        c.start()
        forwards.append(c)
        c = remote(piece, piece, fwd_ss.at[j], fwd_rs.at[p], partner)
        c.start()
        forwards.append(c)

    lax.fori_loop(2, 4, front, 0)

    for j in range(4):
        p = ((zpos + j) % 4) * 2 + 1 - ypos
        piece = conv_all.at[p, core]
        remote(piece, piece, conv_ss.at[0], conv_rs.at[p], ypeer).wait_recv()
        c = remote(piece, piece, fwd_ss.at[4 + j], fwd_rs.at[p], partner)
        c.start()
        forwards.append(c)
    own.wait()
    for j in range(1, 8):
        p = (dp + j) % 8
        other = conv_all.at[p, 1 - core]
        remote(other, other, fwd_ss.at[j], fwd_rs.at[p], partner).wait_recv()

    def middle(r, _):
        all_rows = pl.ds(pl.multiple_of(r * 256, 256), 256)
        second[...] = lax.dot_general(
            taps[all_rows, :],
            conv_all[...].reshape(512, 1536),
            (((1,), (1,)), ((), ())),
            preferred_element_type=F32,
        )
        count2 = jnp.floor((counts[r] - 2.5) * 0.5) + 1.0

        def activate(i, _):
            valid = frame_ids(i) < count2
            value = second[chunk(i)]
            phi, grad = phi_and_slope(value)
            feat_rows[r, chunk(i)] = jnp.where(valid, value * phi, 0.0).astype(BF16)
            rows = pl.ds(pl.multiple_of(r * 256 + i * STEP, STEP), STEP)
            delta[rows, :] = jnp.where(valid, cot_rows[r, chunk(i)].astype(F32) * grad, 0.0).astype(BF16)
            return 0

        lax.fori_loop(0, steps, activate, 0)
        return 0

    lax.fori_loop(0, 4, middle, 0)

    stage = {}

    def weight_grad(b):
        def rows_of(m, _):
            cols = pl.ds(pl.multiple_of(m * 128, 128), 128)
            part = lax.dot_general(
                delta[:, cols],
                taps[:, b * WIDTH : (b + 1) * WIDTH],
                (((0,), (0,)), ((), ())),
                preferred_element_type=F32,
            ).reshape(2, 2, 2, 16, WIDTH)
            gc_full[b, pl.ds(m * 2, 2)] = part
            gc_send[b, pl.ds(m * 2, 2)] = part.astype(BF16)
            return 0

        lax.fori_loop(0, 4, rows_of, 0)
        stage[b, 0] = remote(gc_send.at[b, :, :, 1 - core], gc_r1.at[b], st_ss.at[b, 0], st_rs.at[b, 0], partner)
        stage[b, 0].start()

    def reduce_first(b):
        stage[b, 0].wait()

        def one(i, _):
            if b % 2 == 0:
                keep, give = (i, xpos), (i, 1 - xpos)
            else:
                keep, give = ((i // 2) * 2 + ypos, i % 2), ((i // 2) * 2 + 1 - ypos, i % 2)
            gc_k2[b, i] = gc_full[b, keep[0], keep[1], core] + gc_r1[b, keep[0], keep[1]].astype(F32)
            gc_s2[b, i] = (
                gc_full[b, give[0], give[1], core] + gc_r1[b, give[0], give[1]].astype(F32)
            ).astype(BF16)
            return 0

        lax.fori_loop(0, 8, one, 0)
        peer = xpeer if b % 2 == 0 else ypeer
        stage[b, 1] = remote(gc_s2.at[b], gc_r2.at[b], st_ss.at[b, 1], st_rs.at[b, 1], peer)
        stage[b, 1].start()

    def reduce_second(b):
        stage[b, 1].wait()
        place = ypos if b % 2 == 0 else xpos

        def one(z, _):
            keep, give = z * 2 + place, z * 2 + 1 - place
            gc_k3[b, z] = gc_k2[b, keep] + gc_r2[b, keep].astype(F32)
            gc_s3[b, z] = (gc_k2[b, give] + gc_r2[b, give].astype(F32)).astype(BF16)
            return 0

        lax.fori_loop(0, 4, one, 0)
        peer = ypeer if b % 2 == 0 else xpeer
        stage[b, 2] = remote(gc_s3.at[b], gc_r3.at[b], st_ss.at[b, 2], st_rs.at[b, 2], peer)
        stage[b, 2].start()

    late_sends = []

    def reduce_third(b):
        stage[b, 2].wait()

        def one(z, _):
            total = gc_k3[b, z] + gc_r3[b, z].astype(F32)
            gc_k4[b, z] = total
            gc_s4[b, z] = total.astype(BF16)
            return 0

        lax.fori_loop(0, 4, one, 0)
        for j in range(1, 4):
            zp = (zpos + j) % 4
            c = remote(
                gc_s4.at[b, zp], gc_r4.at[b, zpos], z_ss.at[b, j], z_rs.at[b, zpos], (zp * 2 + ypos, grp)
            )
            c.start()
            late_sends.append(c)

    def reduce_last(b):
        total = gc_k4[b, zpos]
        for j in range(1, 4):
            zp = (zpos + j) % 4
            piece = gc_r4.at[b, zp]
            remote(piece, piece, z_ss.at[b, j], z_rs.at[b, zp], (zp * 2 + ypos, grp)).wait_recv()
            total = total + gc_r4[b, zp].astype(F32)
        gc_out[b, grp] = total.astype(BF16)
        for j in range(1, 4):
            c = remote(
                gc_out.at[b, grp], gc_out.at[b, grp], out_ss.at[b, j], out_rs.at[b, grp], (dp, (grp + j) % 4)
            )
            c.start()
            late_sends.append(c)

    def gathered(b):
        for j in range(1, 4):
            p = (grp + j) % 4
            piece = gc_out.at[b, p]
            remote(piece, piece, out_ss.at[b, j], out_rs.at[b, p], (dp, p)).wait_recv()
        gconv_ref[:, b * WIDTH : (b + 1) * WIDTH] = gc_out[b].astype(F32).reshape(64, WIDTH)

    def backward(r):
        rows = slice(r * 256, r * 256 + 256)
        weights = conv_all[...].reshape(512, 1536)
        part = lax.dot_general(
            delta[rows, :], weights[:, 0:1024], (((1,), (0,)), ((), ())), preferred_element_type=F32
        )
        back[8:264, :] = part
        even_rows[0:8] = jnp.zeros((8, 512), F32)
        even_rows[8:264] = lax.dot_general(
            delta[rows, :], weights[:, 1024:1536], (((1,), (0,)), ((), ())), preferred_element_type=F32
        )
        back[8:264, 0:512] = back[8:264, 0:512] + even_rows[7:263]
        count, inv, gain = counts[r], inv_all[r], gain_ref[...]
        inv_count = 1.0 / count

        def shifted_chunk(i):
            return pl.ds(pl.multiple_of(i * STEP + 8, 8), STEP)

        def norm_sums(i, carry):
            plain, cross = carry
            even = back[shifted_chunk(i), 0:512] * slope[r, chunk(i), 0:512]
            odd = back[shifted_chunk(i), 512:1024] * slope[r, chunk(i), 512:1024]
            back[shifted_chunk(i), 0:512] = even
            back[shifted_chunk(i), 512:1024] = odd
            both = even * normed[r, chunk(i), 0:512] + odd * normed[r, chunk(i), 512:1024]
            return plain + fold_rows(even + odd), cross + fold_rows(both)

        zero = jnp.zeros((8, 512), F32)
        plain, cross = lax.fori_loop(0, steps, norm_sums, (zero, zero))
        plain = jnp.sum(plain, axis=0, keepdims=True)
        cross = jnp.sum(cross, axis=0, keepdims=True)
        sums[0:1] = sums[0:1] + cross
        sums[1:2] = sums[1:2] + plain
        mean_grad = plain * gain * inv_count
        mean_cross = cross * gain * inv_count

        def first_delta(i, _):
            ids = frame_ids(i) * 2.0
            for half in range(2):
                cols = slice(half * 512, half * 512 + 512)
                value = back[shifted_chunk(i), cols] * gain - mean_grad
                value = (value - normed[r, chunk(i), cols] * mean_cross) * inv
                dfirst[chunk(i), cols] = jnp.where(ids + float(half) < count, value, 0.0).astype(BF16)
            return 0

        lax.fori_loop(0, steps, first_delta, 0)
        first_acc[...] += lax.dot_general(
            lhs_all[r], dfirst[...], (((1,), (0,)), ((), ())), preferred_element_type=F32
        )

    weight_grad(0)
    weight_grad(1)
    weight_grad(2)
    weight_grad(3)
    reduce_first(0)
    reduce_first(1)

    def join_rows(i, _):
        parts = [feat_rows[r, chunk(i)].astype(F32) for r in range(4)]
        feat_wide[chunk(i)] = jnp.stack(parts, axis=1).astype(BF16)
        return 0

    lax.fori_loop(0, steps, join_rows, 0)
    feat_out = pltpu.make_async_copy(feat_wide.at[0:255], feat_ref, feat_sem)
    feat_out.start()
    backward(0)
    reduce_first(2)
    reduce_first(3)
    backward(1)
    backward(2)
    reduce_second(0)
    reduce_second(1)
    backward(3)

    small = sm_grp.at[grp]
    small[0:10] = first_acc[0:10, 0:512]
    small[0:5] = small[0:5] + first_acc[5:10, 512:1024]
    small[5:10] = small[5:10] + first_acc[16:21, 512:1024]
    small[10:12] = sums[0:2]
    small[12:16] = jnp.zeros((4, 512), F32)
    for j in range(1, 4):
        c = remote(sm_grp.at[grp], sm_grp.at[grp], sg_ss.at[j], sg_rs.at[grp], (dp, (grp + j) % 4))
        c.start()
        late_sends.append(c)

    reduce_third(0)
    reduce_third(1)

    for j in range(1, 4):
        p = (grp + j) % 4
        remote(sm_grp.at[p], sm_grp.at[p], sg_ss.at[j], sg_rs.at[p], (dp, p)).wait_recv()
    sm_y[0] = (sm_grp[0] + sm_grp[1]) + (sm_grp[2] + sm_grp[3])
    sy = remote(sm_y.at[0], sm_y.at[1], sy_ss, sy_rs, ypeer)
    sy.start()

    reduce_second(2)
    reduce_second(3)
    sy.wait()
    sm_z[zpos] = sm_y[0] + sm_y[1]
    for j in range(1, 4):
        zp = (zpos + j) % 4
        c = remote(sm_z.at[zpos], sm_z.at[zpos], sz_ss.at[j], sz_rs.at[zpos], (zp * 2 + ypos, grp))
        c.start()
        late_sends.append(c)
    reduce_third(2)
    reduce_third(3)
    for b in range(4):
        reduce_last(b)
    for j in range(1, 4):
        zp = (zpos + j) % 4
        remote(sm_z.at[zp], sm_z.at[zp], sz_ss.at[j], sz_rs.at[zp], (zp * 2 + ypos, grp)).wait_recv()
    small_sum = (sm_z[0] + sm_z[1]) + (sm_z[2] + sm_z[3])
    ggain_ref[...] = small_sum[10:11]
    gbias_ref[...] = small_sum[11:12]
    gfirst_ref[...] = pltpu.roll(small_sum, (8 - dp) % 8 * 64, 1)[0:10, 0:64]
    for b in range(4):
        gathered(b)
    feat_out.wait()
    for c in row_sends + first_sends + conv_sends + forwards + late_sends:
        c.wait_send()


def local_fused(
    waveform, lengths, packing, first_weight, norm_gain, norm_bias, conv_weight, grad_features
):
    dp = lax.axis_index("dp")
    masked = jnp.where(jnp.arange(2560)[None, :] < lengths[:, None], waveform, jnp.zeros_like(waveform))
    blocks = masked.reshape(4, 256, 10).transpose(0, 2, 1)
    notes = jnp.stack([packing, lengths // 16, lengths % 16], axis=1).astype(BF16)
    notes = jnp.broadcast_to(notes[:, :, None], (4, 3, 256))
    wave_rows = jnp.concatenate([blocks, notes, jnp.zeros((4, 3, 256), BF16)], axis=1)
    turned = first_weight.T
    gap = lambda rows: jnp.zeros((rows, 64), BF16)
    stacked = jnp.concatenate(
        [turned, gap(6), gap(5), turned[0:5], gap(6), turned[5:10], gap(11)], axis=0
    )
    odd_half = dp % 2 == 1
    blank = jnp.zeros_like(stacked)
    first_rows = jnp.concatenate(
        [jnp.where(odd_half, blank, stacked), jnp.where(odd_half, stacked, blank)], axis=1
    )
    vmem = lambda *shape: pltpu.VMEM(shape, F32)
    vmem16 = lambda *shape: pltpu.VMEM(shape, BF16)
    dma = pltpu.SemaphoreType.DMA
    features, grad_conv, grad_first, grad_gain, grad_bias = pl.pallas_call(
        fused_kernel,
        out_shape=(
            jax.ShapeDtypeStruct((255, 4, 512), BF16),
            jax.ShapeDtypeStruct((64, 1536), F32),
            jax.ShapeDtypeStruct((10, 64), F32),
            jax.ShapeDtypeStruct((1, 512), F32),
            jax.ShapeDtypeStruct((1, 512), F32),
        ),
        in_specs=[pl.BlockSpec(memory_space=pltpu.VMEM)] * 5 + [pl.BlockSpec(memory_space=pl.ANY)],
        out_specs=[pl.BlockSpec(memory_space=pl.ANY)] + [pl.BlockSpec(memory_space=pltpu.VMEM)] * 4,
        scratch_shapes=[
            vmem16(4, 4, 16, 256), vmem16(8, 48, 128), vmem16(32, 1024), vmem16(8, 2, 32, 1536),
            vmem(4, 256, 1024), vmem(4, 256, 1024), vmem16(1024, 1536), vmem(264, 512),
            vmem16(1024, 512), vmem(256, 512),
            vmem16(256, 4, 512), vmem16(4, 256, 512), vmem16(256, 4, 512), vmem16(4, 256, 512), vmem16(4, 32, 256), vmem(4, 1, 512), vmem(4, 1, 512),
            vmem(264, 1024), vmem16(256, 1024), vmem(32, 1024), vmem(8, 512),
            vmem(4, 8, 2, 2, 16, WIDTH), vmem16(4, 8, 2, 2, 16, WIDTH), vmem16(4, 8, 2, 16, WIDTH),
            vmem(4, 8, 16, WIDTH), vmem16(4, 8, 16, WIDTH), vmem16(4, 8, 16, WIDTH),
            vmem(4, 4, 16, WIDTH), vmem16(4, 4, 16, WIDTH), vmem16(4, 4, 16, WIDTH),
            vmem(4, 4, 16, WIDTH), vmem16(4, 4, 16, WIDTH), vmem16(4, 4, 16, WIDTH),
            vmem16(4, 4, 16, WIDTH),
            vmem(4, 16, 512), vmem(2, 16, 512), vmem(4, 16, 512),
            dma((4,)), dma((4,)), dma((8,)), dma((8,)), dma((8,)), dma((8,)), dma((8,)), dma((8,)), dma, dma, dma,
            dma((4, 3)), dma((4, 3)), dma((4, 4)), dma((4, 4)), dma((4, 4)), dma((4, 4)), dma((4,)), dma((4,)),
            dma, dma, dma((4,)), dma((4,)),
        ],
        compiler_params=pltpu.CompilerParams(
            collective_id=0, has_side_effects=True, vmem_limit_bytes=60 * 1024 * 1024
        ),
    )(wave_rows, first_rows, conv_weight.reshape(2, 32, 1536), norm_gain[None], norm_bias[None], grad_features.transpose(1, 0, 2))
    return (features.transpose(1, 0, 2), grad_conv, grad_first.T, grad_gain[0], grad_bias[0])


def solution(mesh):
    shape = dict(mesh.shape)
    fused = shape["dp"] == 8 and shape["group"] == 4
    return jax.shard_map(
        local_fused if fused else local,
        mesh=mesh,
        in_specs=(
            P(("dp", "group"), None),
            P(("dp", "group")),
            P(("dp", "group")),
            P("dp", None),
            P(),
            P(),
            P("dp", None),
            P(("dp", "group"), None, None),
        ),
        out_specs=(P(("dp", "group"), None, None), P("dp", None), P("dp", None), P(), P()),
        check_vma=False,
    )
```

```python
import functools

import jax
import jax.numpy as jnp
from jax import lax
from jax.experimental import pallas as pl
from jax.experimental.pallas import tpu as pltpu
from jax.sharding import PartitionSpec as P

MESH = pl.DeviceIdType.MESH
F32, BF16 = jnp.float32, jnp.bfloat16
STEP = 32


def gelu_slope(values):
    return (
        0.5 * (1.0 + lax.erf(values * 0.7071067811865476))
        + values * jnp.exp(-0.5 * values * values) * 0.3989422804014327
    )


def tap_matrix(hidden, frames_second):
    row_count, frames_first, channels = hidden.shape
    zero_frame = jnp.zeros((row_count, 1, channels), hidden.dtype)
    paired = jnp.concatenate([hidden, zero_frame], axis=1).reshape(
        row_count, frames_second + 1, 2, channels
    )
    even_half = paired[:, :, 0]
    odd_half = paired[:, :, 1]
    stacked = jnp.concatenate(
        [even_half[:, :frames_second], odd_half[:, :frames_second], even_half[:, 1:]], axis=2
    )
    return stacked.reshape(row_count * frames_second, 3 * channels)


def spread_back(back_taps, row_count, frames_second, frames_first):
    first_tap = back_taps[0].reshape(row_count, frames_second, -1)
    middle_tap = back_taps[1].reshape(row_count, frames_second, -1)
    last_tap = back_taps[2].reshape(row_count, frames_second, -1)
    channels = first_tap.shape[2]
    zero_frame = jnp.zeros((row_count, 1, channels), jnp.float32)
    even_half = jnp.concatenate([first_tap, zero_frame], axis=1) + jnp.concatenate(
        [zero_frame, last_tap], axis=1
    )
    odd_half = jnp.concatenate([middle_tap, zero_frame], axis=1)
    joined = jnp.stack([even_half, odd_half], axis=2).reshape(
        row_count, 2 * frames_second + 2, channels
    )
    return joined[:, :frames_first]


def local(
    waveform, lengths, packing, first_weight, norm_gain, norm_bias, conv_weight, grad_features
):
    row_count, capacity = waveform.shape
    channels = norm_gain.shape[0]
    frames_first = capacity // 5 - 1
    frames_second = (capacity // 5 - 2) // 2
    groups = lax.axis_size("group")
    own_group = lax.axis_index("group")
    group_rows = groups * row_count
    all_pack, all_lengths = (
        lax.all_gather(packing, "group", axis=0, tiled=True),
        lax.all_gather(lengths, "group", axis=0, tiled=True),
    )
    target = all_pack // row_count
    slot_index = all_pack % row_count
    positions = jnp.arange(group_rows)
    source = positions // row_count
    same_source = source[:, None] == source[None, :]
    same_target = target[:, None] == target[None, :]
    before = positions[:, None] > positions[None, :]
    rank_among = jnp.sum((same_source & same_target & before).astype(jnp.int32), axis=1)
    arriving = target == own_group
    slot_ids = jnp.arange(row_count)
    choose_slot = (slot_index[None, :] == slot_ids[:, None]) & arriving[None, :]
    local_lengths = jnp.sum(jnp.where(choose_slot, all_lengths[None, :], 0), axis=1)
    per_peer = 2 * ((row_count + 2 * groups - 1) // (2 * groups))
    lane_ids = jnp.arange(per_peer)
    own_target = lax.dynamic_slice_in_dim(target, own_group * row_count, row_count)
    own_rank = lax.dynamic_slice_in_dim(rank_among, own_group * row_count, row_count)
    outgoing = (
        (own_target[None, None, :] == jnp.arange(groups)[:, None, None])
        & (own_rank[None, None, :] == lane_ids[None, :, None])
    ).astype(jnp.bfloat16)
    send_rows = jnp.einsum(
        "gkr,rs->gks", outgoing, waveform, preferred_element_type=jnp.float32
    ).astype(jnp.bfloat16)
    received = lax.all_to_all(send_rows, "group", split_axis=0, concat_axis=0, tiled=True)
    pick_slots = (
        choose_slot[:, :, None] & (rank_among[None, :, None] == lane_ids[None, None, :])
    ).astype(jnp.float32)
    pick_slots = jnp.sum(pick_slots.reshape(row_count, groups, row_count, per_peer), axis=2).astype(
        jnp.bfloat16
    )
    wave_rows = jnp.einsum(
        "lsk,skn->ln", pick_slots, received, preferred_element_type=jnp.float32
    ).astype(jnp.bfloat16)
    first_whole = lax.all_gather(first_weight, "dp", axis=0, tiled=True)
    in_length = jnp.arange(capacity)[None, :] < local_lengths[:, None]
    masked = jnp.where(in_length, wave_rows, jnp.zeros_like(wave_rows))
    blocks = masked.reshape(row_count, capacity // 5, 5)
    taps_first = jnp.concatenate([blocks[:, :-1], blocks[:, 1:]], axis=2).reshape(
        row_count * frames_first, 10
    )
    conv_first = lax.dot_general(
        taps_first, first_whole, (((1,), (1,)), ((), ())), preferred_element_type=jnp.float32
    )
    conv_first = conv_first.reshape(row_count, frames_first, channels)
    count_first = (local_lengths - 10) // 5 + 1
    count_second = (count_first - 3) // 2 + 1
    valid_first = (jnp.arange(frames_first)[None, :] < count_first[:, None]).astype(jnp.float32)[
        :, :, None
    ]
    valid_second = (jnp.arange(frames_second)[None, :] < count_second[:, None]).astype(jnp.float32)[
        :, :, None
    ]
    count_float = count_first.astype(jnp.float32)[:, None, None]
    row_mean = jnp.sum(conv_first * valid_first, axis=1, keepdims=True) / count_float
    centred = (conv_first - row_mean) * valid_first
    row_var = jnp.sum(centred * centred, axis=1, keepdims=True) / count_float
    inv_scale = lax.rsqrt(row_var + 1e-05)
    normed = (conv_first - row_mean) * inv_scale
    shifted = normed * norm_gain + norm_bias
    hidden = (jax.nn.gelu(shifted, approximate=False) * valid_first).astype(jnp.bfloat16)
    taps_second = tap_matrix(hidden, frames_second)
    conv_whole = lax.all_gather(conv_weight, "dp", axis=0, tiled=True)
    conv_second = lax.dot_general(
        taps_second, conv_whole, (((1,), (1,)), ((), ())), preferred_element_type=jnp.float32
    )
    conv_second = conv_second.reshape(row_count, frames_second, channels)
    features = (jax.nn.gelu(conv_second, approximate=False) * valid_second).astype(jnp.bfloat16)
    delta_second = (
        grad_features.astype(jnp.float32) * valid_second * gelu_slope(conv_second)
    ).astype(jnp.bfloat16)
    delta_flat = delta_second.reshape(row_count * frames_second, channels)
    back_taps = tuple(
        (
            jnp.dot(
                delta_flat,
                conv_whole[:, tap_index * channels : (tap_index + 1) * channels],
                preferred_element_type=jnp.float32,
            )
            for tap_index in range(3)
        )
    )
    share = lax.psum_scatter(
        lax.dot_general(
            delta_flat, taps_second, (((0,), (0,)), ((), ())), preferred_element_type=jnp.float32
        ),
        "dp",
        scatter_dimension=0,
        tiled=True,
    )
    grad_conv = lax.psum(share, "group")
    delta_hidden = spread_back(back_taps, row_count, frames_second, frames_first)
    delta_norm = delta_hidden * valid_first * gelu_slope(shifted)
    gain_term = jnp.sum(delta_norm * normed, axis=(0, 1))
    bias_term = jnp.sum(delta_norm, axis=(0, 1))
    scaled = delta_norm * norm_gain
    mean_grad = jnp.sum(scaled, axis=1, keepdims=True) / count_float
    mean_cross = jnp.sum(scaled * normed, axis=1, keepdims=True) / count_float
    delta_first = ((scaled - mean_grad - normed * mean_cross) * inv_scale * valid_first).astype(
        jnp.bfloat16
    )
    first_term = lax.dot_general(
        delta_first.reshape(row_count * frames_first, channels),
        taps_first,
        (((0,), (0,)), ((), ())),
        preferred_element_type=jnp.float32,
    )
    stacked = jnp.concatenate([first_term, gain_term[:, None], bias_term[:, None]], axis=1)
    summed = lax.psum(stacked, ("dp", "group"))
    shard_rows = channels // lax.axis_size("dp")
    grad_first = lax.dynamic_slice_in_dim(
        summed[:, :10], lax.axis_index("dp") * shard_rows, shard_rows, 0
    )
    return (features, grad_conv, grad_first, summed[:, 10], summed[:, 11])


WIDTH = 384


def phi_and_slope(values):
    phi = 0.5 * (1.0 + lax.erf(values * 0.7071067811865476))
    return phi, phi + values * jnp.exp(-0.5 * values * values) * 0.3989422804014327


def fold_rows(block):
    return jnp.sum(block.reshape(block.shape[0] // 8, 8, block.shape[1]), axis=0)


def fused_kernel(
    wave_ref, first_ref, conv_ref, gain_ref, bias_ref, cot_ref,
    feat_ref, gconv_ref, gfirst_ref, ggain_ref, gbias_ref,
    rows_all, first_all, first_both, conv_all, normed, slope, taps, even_rows, delta, second,
    cot_wide, cot_rows, feat_wide, feat_rows, lhs_all, counts, inv_all, back, dfirst, first_acc, sums,
    gc_full, gc_send, gc_r1, gc_k2, gc_s2, gc_r2, gc_k3, gc_s3, gc_r3, gc_k4, gc_s4, gc_r4, gc_out,
    sm_grp, sm_y, sm_z,
    row_ss, row_rs, first_ss, first_rs, conv_ss, conv_rs, fwd_ss, fwd_rs, own_sem, cot_sem, feat_sem,
    st_ss, st_rs, z_ss, z_rs, out_ss, out_rs, sg_ss, sg_rs, sy_ss, sy_rs, sz_ss, sz_rs,
):
    dp, grp = lax.axis_index("dp"), lax.axis_index("group")
    core, xpos = grp % 2, grp // 2
    ypos, zpos = dp % 2, dp // 2
    partner = (dp, xpos * 2 + (1 - core))
    xpeer = (dp, (1 - xpos) * 2 + core)
    ypeer = (zpos * 2 + (1 - ypos), grp)

    def chunk(i):
        return pl.ds(pl.multiple_of(i * STEP, STEP), STEP)

    def frame_ids(i):
        ids = lax.broadcasted_iota(jnp.int32, (STEP, 512), 0) + i * STEP
        return ids.astype(F32)

    steps = 256 // STEP

    def remote(src, dst, ss, rs, dev):
        return pltpu.make_async_remote_copy(
            src_ref=src, dst_ref=dst, send_sem=ss, recv_sem=rs, device_id=dev, device_id_type=MESH
        )

    cot_in = pltpu.make_async_copy(cot_ref, cot_wide.at[0:255], cot_sem)
    cot_in.start()
    barrier = pltpu.get_barrier_semaphore()
    for j in range(1, 4):
        pl.semaphore_signal(barrier, inc=1, device_id=(dp, (grp + j) % 4), device_id_type=MESH)
    for j in range(1, 8):
        pl.semaphore_signal(barrier, inc=1, device_id=((dp + j) % 8, grp), device_id_type=MESH)
    cot_wide[255] = jnp.zeros((4, 512), BF16)
    even_rows[256:264] = jnp.zeros((8, 512), F32)
    first_acc[...] = jnp.zeros_like(first_acc)
    sums[...] = jnp.zeros_like(sums)
    cot_in.wait()

    def split_rows(i, _):
        block = cot_wide[chunk(i)].astype(F32)
        for r in range(4):
            cot_rows[r, chunk(i)] = block[:, r, :].astype(BF16)
        return 0

    lax.fori_loop(0, steps, split_rows, 0)
    pl.semaphore_wait(barrier, 10)

    row_sends = []
    for j in range(1, 4):
        c = remote(wave_ref, rows_all.at[grp], row_ss.at[j], row_rs.at[grp], (dp, (grp + j) % 4))
        c.start()
        row_sends.append(c)
    first_sends, conv_sends = [], []
    for j in range(1, 8):
        c = remote(first_ref, first_all.at[dp], first_ss.at[j], first_rs.at[dp], ((dp + j) % 8, grp))
        c.start()
        first_sends.append(c)
    for j in range(1, 4):
        peer = (((zpos + j) % 4) * 2 + ypos, grp)
        c = remote(conv_ref.at[core], conv_all.at[dp, core], conv_ss.at[j], conv_rs.at[dp], peer)
        c.start()
        conv_sends.append(c)
    c = remote(conv_ref.at[core], conv_all.at[dp, core], conv_ss.at[0], conv_rs.at[dp], ypeer)
    c.start()
    conv_sends.append(c)
    own = pltpu.make_async_copy(conv_ref, conv_all.at[dp], own_sem)
    own.start()
    rows_all[grp] = wave_ref[...]
    first_all[dp] = first_ref[...]

    for j in range(1, 4):
        p = (grp + j) % 4
        remote(wave_ref, rows_all.at[p], row_ss.at[j], row_rs.at[p], (dp, p)).wait_recv()
    for j in range(1, 8):
        p = (dp + j) % 8
        remote(first_ref, first_all.at[p], first_ss.at[j], first_rs.at[p], (p, grp)).wait_recv()

    for b in range(4):
        joined = first_all[2 * b] + first_all[2 * b + 1]
        lanes = slice(b * 128, b * 128 + 128)
        first_both[0:16, lanes] = joined[0:16]
        first_both[16:32, lanes] = jnp.zeros((16, 128), BF16)
        first_both[:, 512 + b * 128 : 640 + b * 128] = joined[16:48]

    def front(r, _):
        place = (grp * 4 + r).astype(F32)
        chosen = jnp.zeros((16, 256), F32)
        for s in range(4):
            for i in range(4):
                row = rows_all[s, i].astype(F32)
                chosen = chosen + row * (row[10:11] == place).astype(F32)
        lhs_all[r, 0:16] = chosen.astype(BF16)
        lhs_all[r, 16:32] = pltpu.roll(chosen, 255, 1).astype(BF16)
        length = chosen[11:12] * 16.0 + chosen[12:13]
        length = jnp.concatenate([length, length], axis=1)
        count = jnp.floor((length - 9.5) * 0.2) + 1.0
        counts[r] = count
        normed[r] = lax.dot_general(
            lhs_all[r], first_both[...], (((0,), (0,)), ((), ())), preferred_element_type=F32
        )
        inv_count = 1.0 / count

        def add_up(i, acc):
            ids = frame_ids(i) * 2.0
            even = jnp.where(ids < count, normed[r, chunk(i), 0:512], 0.0)
            odd = jnp.where(ids + 1.0 < count, normed[r, chunk(i), 512:1024], 0.0)
            return acc + fold_rows(even + odd)

        total = lax.fori_loop(0, steps, add_up, jnp.zeros((8, 512), F32))
        mean = jnp.sum(total, axis=0, keepdims=True) * inv_count

        def add_squares(i, acc):
            ids = frame_ids(i) * 2.0
            even = jnp.where(ids < count, normed[r, chunk(i), 0:512] - mean, 0.0)
            odd = jnp.where(ids + 1.0 < count, normed[r, chunk(i), 512:1024] - mean, 0.0)
            return acc + fold_rows(even * even + odd * odd)

        total = lax.fori_loop(0, steps, add_squares, jnp.zeros((8, 512), F32))
        inv = lax.rsqrt(jnp.sum(total, axis=0, keepdims=True) * inv_count + 1e-05)
        inv_all[r] = inv
        gain, bias = gain_ref[...], bias_ref[...]

        def activate(i, _):
            ids = frame_ids(i) * 2.0
            rows = pl.ds(pl.multiple_of(r * 256 + i * STEP, STEP), STEP)
            for half in range(2):
                cols = slice(half * 512, half * 512 + 512)
                valid = ids + float(half) < count
                value = (normed[r, chunk(i), cols] - mean) * inv
                normed[r, chunk(i), cols] = value
                shifted = value * gain + bias
                phi, grad = phi_and_slope(shifted)
                hidden = jnp.where(valid, shifted * phi, 0.0)
                slope[r, chunk(i), cols] = jnp.where(valid, grad, 0.0)
                taps[rows, cols] = hidden.astype(BF16)
                if half == 0:
                    even_rows[chunk(i)] = hidden
            return 0

        lax.fori_loop(0, steps, activate, 0)
        all_rows = pl.ds(pl.multiple_of(r * 256, 256), 256)
        taps[all_rows, 1024:1536] = even_rows[1:257].astype(BF16)
        return 0

    lax.fori_loop(0, 2, front, 0)

    forwards = []
    for j in range(1, 4):
        p = ((zpos + j) % 4) * 2 + ypos
        piece = conv_all.at[p, core]
        remote(piece, piece, conv_ss.at[j], conv_rs.at[p], (p, grp)).wait_recv()
        c = remote(piece, piece, conv_ss.at[3 + j], conv_rs.at[p], ypeer)
        c.start()
        forwards.append(c)
        c = remote(piece, piece, fwd_ss.at[j], fwd_rs.at[p], partner)
        c.start()
        forwards.append(c)

    lax.fori_loop(2, 4, front, 0)

    for j in range(4):
        p = ((zpos + j) % 4) * 2 + 1 - ypos
        piece = conv_all.at[p, core]
        remote(piece, piece, conv_ss.at[0], conv_rs.at[p], ypeer).wait_recv()
        c = remote(piece, piece, fwd_ss.at[4 + j], fwd_rs.at[p], partner)
        c.start()
        forwards.append(c)
    own.wait()
    for j in range(1, 8):
        p = (dp + j) % 8
        other = conv_all.at[p, 1 - core]
        remote(other, other, fwd_ss.at[j], fwd_rs.at[p], partner).wait_recv()

    def middle(r, _):
        all_rows = pl.ds(pl.multiple_of(r * 256, 256), 256)
        second[...] = lax.dot_general(
            taps[all_rows, :],
            conv_all[...].reshape(512, 1536),
            (((1,), (1,)), ((), ())),
            preferred_element_type=F32,
        )
        count2 = jnp.floor((counts[r] - 2.5) * 0.5) + 1.0

        def activate(i, _):
            valid = frame_ids(i) < count2
            value = second[chunk(i)]
            phi, grad = phi_and_slope(value)
            feat_rows[r, chunk(i)] = jnp.where(valid, value * phi, 0.0).astype(BF16)
            rows = pl.ds(pl.multiple_of(r * 256 + i * STEP, STEP), STEP)
            delta[rows, :] = jnp.where(valid, cot_rows[r, chunk(i)].astype(F32) * grad, 0.0).astype(BF16)
            return 0

        lax.fori_loop(0, steps, activate, 0)
        return 0

    lax.fori_loop(0, 4, middle, 0)

    stage = {}

    def weight_grad(b):
        def rows_of(m, _):
            cols = pl.ds(pl.multiple_of(m * 128, 128), 128)
            part = lax.dot_general(
                delta[:, cols],
                taps[:, b * WIDTH : (b + 1) * WIDTH],
                (((0,), (0,)), ((), ())),
                preferred_element_type=F32,
            ).reshape(2, 2, 2, 16, WIDTH)
            gc_full[b, pl.ds(m * 2, 2)] = part
            gc_send[b, pl.ds(m * 2, 2)] = part.astype(BF16)
            return 0

        lax.fori_loop(0, 4, rows_of, 0)
        stage[b, 0] = remote(gc_send.at[b, :, :, 1 - core], gc_r1.at[b], st_ss.at[b, 0], st_rs.at[b, 0], partner)
        stage[b, 0].start()

    def reduce_first(b):
        stage[b, 0].wait()

        def one(i, _):
            if b % 2 == 0:
                keep, give = (i, xpos), (i, 1 - xpos)
            else:
                keep, give = ((i // 2) * 2 + ypos, i % 2), ((i // 2) * 2 + 1 - ypos, i % 2)
            gc_k2[b, i] = gc_full[b, keep[0], keep[1], core] + gc_r1[b, keep[0], keep[1]].astype(F32)
            gc_s2[b, i] = (
                gc_full[b, give[0], give[1], core] + gc_r1[b, give[0], give[1]].astype(F32)
            ).astype(BF16)
            return 0

        lax.fori_loop(0, 8, one, 0)
        peer = xpeer if b % 2 == 0 else ypeer
        stage[b, 1] = remote(gc_s2.at[b], gc_r2.at[b], st_ss.at[b, 1], st_rs.at[b, 1], peer)
        stage[b, 1].start()

    def reduce_second(b):
        stage[b, 1].wait()
        place = ypos if b % 2 == 0 else xpos

        def one(z, _):
            keep, give = z * 2 + place, z * 2 + 1 - place
            gc_k3[b, z] = gc_k2[b, keep] + gc_r2[b, keep].astype(F32)
            gc_s3[b, z] = (gc_k2[b, give] + gc_r2[b, give].astype(F32)).astype(BF16)
            return 0

        lax.fori_loop(0, 4, one, 0)
        peer = ypeer if b % 2 == 0 else xpeer
        stage[b, 2] = remote(gc_s3.at[b], gc_r3.at[b], st_ss.at[b, 2], st_rs.at[b, 2], peer)
        stage[b, 2].start()

    late_sends = []

    def reduce_third(b):
        stage[b, 2].wait()

        def one(z, _):
            total = gc_k3[b, z] + gc_r3[b, z].astype(F32)
            gc_k4[b, z] = total
            gc_s4[b, z] = total.astype(BF16)
            return 0

        lax.fori_loop(0, 4, one, 0)
        for j in range(1, 4):
            zp = (zpos + j) % 4
            c = remote(
                gc_s4.at[b, zp], gc_r4.at[b, zpos], z_ss.at[b, j], z_rs.at[b, zpos], (zp * 2 + ypos, grp)
            )
            c.start()
            late_sends.append(c)

    def reduce_last(b):
        total = gc_k4[b, zpos]
        for j in range(1, 4):
            zp = (zpos + j) % 4
            piece = gc_r4.at[b, zp]
            remote(piece, piece, z_ss.at[b, j], z_rs.at[b, zp], (zp * 2 + ypos, grp)).wait_recv()
            total = total + gc_r4[b, zp].astype(F32)
        gc_out[b, grp] = total.astype(BF16)
        for j in range(1, 4):
            c = remote(
                gc_out.at[b, grp], gc_out.at[b, grp], out_ss.at[b, j], out_rs.at[b, grp], (dp, (grp + j) % 4)
            )
            c.start()
            late_sends.append(c)

    def gathered(b):
        for j in range(1, 4):
            p = (grp + j) % 4
            piece = gc_out.at[b, p]
            remote(piece, piece, out_ss.at[b, j], out_rs.at[b, p], (dp, p)).wait_recv()
        gconv_ref[:, b * WIDTH : (b + 1) * WIDTH] = gc_out[b].astype(F32).reshape(64, WIDTH)

    def backward(r):
        rows = slice(r * 256, r * 256 + 256)
        weights = conv_all[...].reshape(512, 1536)
        part = lax.dot_general(
            delta[rows, :], weights[:, 0:1024], (((1,), (0,)), ((), ())), preferred_element_type=F32
        )
        back[8:264, :] = part
        even_rows[0:8] = jnp.zeros((8, 512), F32)
        even_rows[8:264] = lax.dot_general(
            delta[rows, :], weights[:, 1024:1536], (((1,), (0,)), ((), ())), preferred_element_type=F32
        )
        back[8:264, 0:512] = back[8:264, 0:512] + even_rows[7:263]
        count, inv, gain = counts[r], inv_all[r], gain_ref[...]
        inv_count = 1.0 / count

        def shifted_chunk(i):
            return pl.ds(pl.multiple_of(i * STEP + 8, 8), STEP)

        def norm_sums(i, carry):
            plain, cross = carry
            even = back[shifted_chunk(i), 0:512] * slope[r, chunk(i), 0:512]
            odd = back[shifted_chunk(i), 512:1024] * slope[r, chunk(i), 512:1024]
            back[shifted_chunk(i), 0:512] = even
            back[shifted_chunk(i), 512:1024] = odd
            both = even * normed[r, chunk(i), 0:512] + odd * normed[r, chunk(i), 512:1024]
            return plain + fold_rows(even + odd), cross + fold_rows(both)

        zero = jnp.zeros((8, 512), F32)
        plain, cross = lax.fori_loop(0, steps, norm_sums, (zero, zero))
        plain = jnp.sum(plain, axis=0, keepdims=True)
        cross = jnp.sum(cross, axis=0, keepdims=True)
        sums[0:1] = sums[0:1] + cross
        sums[1:2] = sums[1:2] + plain
        mean_grad = plain * gain * inv_count
        mean_cross = cross * gain * inv_count

        def first_delta(i, _):
            ids = frame_ids(i) * 2.0
            for half in range(2):
                cols = slice(half * 512, half * 512 + 512)
                value = back[shifted_chunk(i), cols] * gain - mean_grad
                value = (value - normed[r, chunk(i), cols] * mean_cross) * inv
                dfirst[chunk(i), cols] = jnp.where(ids + float(half) < count, value, 0.0).astype(BF16)
            return 0

        lax.fori_loop(0, steps, first_delta, 0)
        first_acc[...] += lax.dot_general(
            lhs_all[r], dfirst[...], (((1,), (0,)), ((), ())), preferred_element_type=F32
        )

    weight_grad(0)
    weight_grad(1)
    reduce_first(0)
    weight_grad(2)
    reduce_first(1)
    weight_grad(3)
    reduce_first(2)

    def join_rows(i, _):
        parts = [feat_rows[r, chunk(i)].astype(F32) for r in range(4)]
        feat_wide[chunk(i)] = jnp.stack(parts, axis=1).astype(BF16)
        return 0

    lax.fori_loop(0, steps, join_rows, 0)
    feat_out = pltpu.make_async_copy(feat_wide.at[0:255], feat_ref, feat_sem)
    feat_out.start()
    backward(0)
    reduce_first(3)
    backward(1)
    reduce_second(0)
    reduce_second(1)
    backward(2)
    backward(3)

    small = sm_grp.at[grp]
    small[0:10] = first_acc[0:10, 0:512]
    small[0:5] = small[0:5] + first_acc[5:10, 512:1024]
    small[5:10] = small[5:10] + first_acc[16:21, 512:1024]
    small[10:12] = sums[0:2]
    small[12:16] = jnp.zeros((4, 512), F32)
    for j in range(1, 4):
        c = remote(sm_grp.at[grp], sm_grp.at[grp], sg_ss.at[j], sg_rs.at[grp], (dp, (grp + j) % 4))
        c.start()
        late_sends.append(c)

    reduce_third(0)
    reduce_third(1)

    for j in range(1, 4):
        p = (grp + j) % 4
        remote(sm_grp.at[p], sm_grp.at[p], sg_ss.at[j], sg_rs.at[p], (dp, p)).wait_recv()
    sm_y[0] = (sm_grp[0] + sm_grp[1]) + (sm_grp[2] + sm_grp[3])
    sy = remote(sm_y.at[0], sm_y.at[1], sy_ss, sy_rs, ypeer)
    sy.start()

    reduce_second(2)
    reduce_second(3)
    sy.wait()
    sm_z[zpos] = sm_y[0] + sm_y[1]
    for j in range(1, 4):
        zp = (zpos + j) % 4
        c = remote(sm_z.at[zpos], sm_z.at[zpos], sz_ss.at[j], sz_rs.at[zpos], (zp * 2 + ypos, grp))
        c.start()
        late_sends.append(c)
    reduce_third(2)
    reduce_third(3)
    for b in range(4):
        reduce_last(b)
    for j in range(1, 4):
        zp = (zpos + j) % 4
        remote(sm_z.at[zp], sm_z.at[zp], sz_ss.at[j], sz_rs.at[zp], (zp * 2 + ypos, grp)).wait_recv()
    small_sum = (sm_z[0] + sm_z[1]) + (sm_z[2] + sm_z[3])
    ggain_ref[...] = small_sum[10:11]
    gbias_ref[...] = small_sum[11:12]
    gfirst_ref[...] = pltpu.roll(small_sum, (8 - dp) % 8 * 64, 1)[0:10, 0:64]
    for b in range(4):
        gathered(b)
    feat_out.wait()
    for c in row_sends + first_sends + conv_sends + forwards + late_sends:
        c.wait_send()


def pass_on(*refs):
    sources, targets, buffers, (in_sem, out_sem) = refs[0:5], refs[5:10], refs[10:15], refs[15:17]
    spans = [(0, pl.ds(0, 64)), (0, pl.ds(64, 64)), (0, pl.ds(128, 64)), (0, pl.ds(192, 63))]
    views = [tuple(group[k].at[span] for group in (sources, buffers, targets)) for k, span in spans]
    views += [(sources[k], buffers[k], targets[k]) for k in range(1, 5)]
    reads, writes = [], []
    for k, (source, buffer, target) in enumerate(views):
        c = pltpu.make_async_copy(source, buffer, in_sem.at[k])
        c.start()
        reads.append(c)
    for k, (source, buffer, target) in enumerate(views):
        reads[k].wait()
        c = pltpu.make_async_copy(buffer, target, out_sem.at[k])
        c.start()
        writes.append(c)
    for c in writes:
        c.wait()


def local_fused(
    waveform, lengths, packing, first_weight, norm_gain, norm_bias, conv_weight, grad_features
):
    dp = lax.axis_index("dp")
    masked = jnp.where(jnp.arange(2560)[None, :] < lengths[:, None], waveform, jnp.zeros_like(waveform))
    blocks = masked.reshape(4, 256, 10).transpose(0, 2, 1)
    notes = jnp.stack([packing, lengths // 16, lengths % 16], axis=1).astype(BF16)
    notes = jnp.broadcast_to(notes[:, :, None], (4, 3, 256))
    wave_rows = jnp.concatenate([blocks, notes, jnp.zeros((4, 3, 256), BF16)], axis=1)
    turned = first_weight.T
    gap = lambda rows: jnp.zeros((rows, 64), BF16)
    stacked = jnp.concatenate(
        [turned, gap(6), gap(5), turned[0:5], gap(6), turned[5:10], gap(11)], axis=0
    )
    odd_half = dp % 2 == 1
    blank = jnp.zeros_like(stacked)
    first_rows = jnp.concatenate(
        [jnp.where(odd_half, blank, stacked), jnp.where(odd_half, stacked, blank)], axis=1
    )
    vmem = lambda *shape: pltpu.VMEM(shape, F32)
    vmem16 = lambda *shape: pltpu.VMEM(shape, BF16)
    dma = pltpu.SemaphoreType.DMA
    features, grad_conv, grad_first, grad_gain, grad_bias = pl.pallas_call(
        fused_kernel,
        out_shape=(
            jax.ShapeDtypeStruct((255, 4, 512), BF16),
            jax.ShapeDtypeStruct((64, 1536), F32),
            jax.ShapeDtypeStruct((10, 64), F32),
            jax.ShapeDtypeStruct((1, 512), F32),
            jax.ShapeDtypeStruct((1, 512), F32),
        ),
        in_specs=[pl.BlockSpec(memory_space=pltpu.VMEM)] * 5 + [pl.BlockSpec(memory_space=pl.ANY)],
        out_specs=[pl.BlockSpec(memory_space=pl.ANY)] + [pl.BlockSpec(memory_space=pltpu.VMEM)] * 4,
        scratch_shapes=[
            vmem16(4, 4, 16, 256), vmem16(8, 48, 128), vmem16(32, 1024), vmem16(8, 2, 32, 1536),
            vmem(4, 256, 1024), vmem(4, 256, 1024), vmem16(1024, 1536), vmem(264, 512),
            vmem16(1024, 512), vmem(256, 512),
            vmem16(256, 4, 512), vmem16(4, 256, 512), vmem16(256, 4, 512), vmem16(4, 256, 512), vmem16(4, 32, 256), vmem(4, 1, 512), vmem(4, 1, 512),
            vmem(264, 1024), vmem16(256, 1024), vmem(32, 1024), vmem(8, 512),
            vmem(4, 8, 2, 2, 16, WIDTH), vmem16(4, 8, 2, 2, 16, WIDTH), vmem16(4, 8, 2, 16, WIDTH),
            vmem(4, 8, 16, WIDTH), vmem16(4, 8, 16, WIDTH), vmem16(4, 8, 16, WIDTH),
            vmem(4, 4, 16, WIDTH), vmem16(4, 4, 16, WIDTH), vmem16(4, 4, 16, WIDTH),
            vmem(4, 4, 16, WIDTH), vmem16(4, 4, 16, WIDTH), vmem16(4, 4, 16, WIDTH),
            vmem16(4, 4, 16, WIDTH),
            vmem(4, 16, 512), vmem(2, 16, 512), vmem(4, 16, 512),
            dma((4,)), dma((4,)), dma((8,)), dma((8,)), dma((8,)), dma((8,)), dma((8,)), dma((8,)), dma, dma, dma,
            dma((4, 3)), dma((4, 3)), dma((4, 4)), dma((4, 4)), dma((4, 4)), dma((4, 4)), dma((4,)), dma((4,)),
            dma, dma, dma((4,)), dma((4,)),
        ],
        compiler_params=pltpu.CompilerParams(
            collective_id=0, has_side_effects=True, vmem_limit_bytes=60 * 1024 * 1024
        ),
    )(wave_rows, first_rows, conv_weight.reshape(2, 32, 1536), norm_gain[None], norm_bias[None], grad_features.transpose(1, 0, 2))
    results = (features, grad_conv, grad_first, grad_gain, grad_bias)
    features, grad_conv, grad_first, grad_gain, grad_bias = pl.pallas_call(
        pass_on,
        out_shape=tuple(jax.ShapeDtypeStruct(each.shape, each.dtype) for each in results),
        in_specs=[pl.BlockSpec(memory_space=pl.ANY)] * 5,
        out_specs=[pl.BlockSpec(memory_space=pl.ANY)] * 5,
        scratch_shapes=[pltpu.VMEM(each.shape, each.dtype) for each in results] + [dma((8,)), dma((8,))],
    )(*results)
    return (features.transpose(1, 0, 2), grad_conv, grad_first.T, grad_gain[0], grad_bias[0])


def solution(mesh):
    shape = dict(mesh.shape)
    fused = shape["dp"] == 8 and shape["group"] == 4
    return jax.shard_map(
        local_fused if fused else local,
        mesh=mesh,
        in_specs=(
            P(("dp", "group"), None),
            P(("dp", "group")),
            P(("dp", "group")),
            P("dp", None),
            P(),
            P(),
            P("dp", None),
            P(("dp", "group"), None, None),
        ),
        out_specs=(P(("dp", "group"), None, None), P("dp", None), P("dp", None), P(), P()),
        check_vma=False,
    )
```
